256 devices in a mesh: dom: 16 (over z, core), mem: 16 (over y, x).
Axes of the slice: x: 4, y: 4, z: 8, core: 2. Of those that a mesh axis runs over, the one named last changes fastest.
Arguments:
- coarse_latents: bfloat16 [16, 8192, 512], P('mem', 'dom'), may hold values from -6 to 6
- send_rows: int32 [16, 16, 128], P('dom'), may hold values from 0 to 511
- up_index: int32 [3, 32768], P(None, 'dom'), may hold values from 0 to 2047
- up_weight: float32 [3, 32768], P(None, 'dom'), may hold values from 0.2 to 1
- neighbors: int32 [6, 32768], P(None, 'dom'), may hold values from 0 to 2303, as said below
- live_counts: int32 [16], P('dom'), may hold values from 1 to 2048, 24576 in all
- area: float32 [32768], P('dom'), may hold values from 0.25 to 4.5
- fine_skip: bfloat16 [32768, 512], P('dom'), may hold values from -6 to 6
- targets: bfloat16 [83, 32768], P(None, 'dom'), may hold values from -6 to 6
- kernel_width: float32 [83], replicated, may hold values from 0.5 to 2
- w_in: bfloat16 [1024, 512], replicated, may hold values from -0.1875 to 0.1875
- w_out: bfloat16 [512, 512], replicated, may hold values from -0.25 to 0.25
- ln_gain: float32 [512], replicated, may hold values from 0.1 to 1.9
- w_head: bfloat16 [512, 83], replicated, may hold values from -0.25 to 0.25
Outputs:
- grad_latent: bfloat16 [16, 32768, 512], P('mem', 'dom')
- grad_head: float32 [16, 512, 83], P('dom')
The draws below stay inside these ranges and needn't reach their ends.
Inputs may be any that keep to these rules, and one draw needn't show every extreme that they name: neighbors[k, p] = 128 + (p % 2048) + e with -128 <= e <= 128.
All inputs are finite; a program needn't handle non-finite values. No bound on the sum of `live_counts` on one device may be relied on, other than what follows from the above.
Results may differ from the reference program's by a relative error of at most 0.015.
The reference program's roundings to bfloat16 on the way count: a program that leaves them out, or rounds other values in their place, can miss the bound.
Values may be sent and summed in bfloat16 or wider, within the bound.
A program may use at most 128 MiB of HBM per device.

```python
import math
import jax
import jax.numpy as jnp
import numpy as np
from jax import lax

H = 512
HID = 512
VARS = 83
K_UP = 3
K_NB = 6
RIM = 128
SLOT = 128
FINE_DEV = 2048
C_DEV = 512
MEMBERS = 16
POINTS = 32768
COARSE = 8192
N_DOM = 16


def draw_neighbors(key, part):
    offsets = jax.random.randint(key, (K_NB, POINTS), -RIM, RIM + 1)
    local = jnp.arange(POINTS, dtype=jnp.int32) % FINE_DEV
    rows = jnp.arange(K_NB, dtype=jnp.int32)[:, None]
    offsets = jnp.where((rows == 0) & (local[None, :] == FINE_DEV - 1), RIM, offsets)
    offsets = jnp.where((rows == 1) & (local[None, :] == 0), -RIM, offsets)
    return (RIM + local[None, :] + offsets).astype(jnp.int32)


def draw_area(key, part):
    rising = 1.0 + 2.0 * jnp.arange(POINTS, dtype=jnp.float32) / POINTS
    rough = jax.random.uniform(key, (POINTS,), jnp.float32, 0.5, 1.5)
    return (rising * rough).astype(jnp.float32)


def touch_ends(drawn, rng, smallest, high):
    longest = drawn.shape.index(max(drawn.shape))
    spots = []
    for shift in (0, 1):
        where = [jax.random.randint(jax.random.fold_in(rng, axis), (), 0, length) for axis, length in enumerate(drawn.shape)]
        where[longest] = (where[longest] + shift) % drawn.shape[longest]
        spots.append(tuple(where))
    return drawn.at[spots[0]].set(smallest).at[spots[1]].set(high)


def block_levels(rng, dims, pieces, least, high):
    def one(position, blocks):
        draws = jax.random.uniform(jax.random.fold_in(jax.random.fold_in(rng, 6), position), (blocks,), jnp.float32, least / len(pieces), high / len(pieces))
        return jnp.repeat(jnp.exp(draws), dims[position] // blocks).reshape((-1,) + (1,) * (len(dims) - position - 1))

    level = one(*pieces[0])
    for cut in pieces[1:]:
        level = level * one(*cut)
    return level


def split_up(count, total, most, lean):
    loads = [(1 << 20) // math.isqrt(rank ** lean) + 1 for rank in range(2, count + 1)]
    rest, counts = total - most - (count - 1), [1] * (count - 1)
    while rest > 0:
        candidates = [i for i in range(count - 1) if counts[i] < most]
        mass, remaining = sum([loads[i] for i in candidates]), rest
        for i in candidates:
            more = min(most - counts[i], max(1, remaining * loads[i] // mass), rest)
            counts[i] = counts[i] + more
            rest = rest - more
    return np.array([most] + counts)


def ragged_sizes(own_key, amount, total, limit, skew):
    if amount == 2:
        one = jax.random.randint(own_key, (), max(1, total - limit), min(limit, total - 1) + 1)
        return jnp.stack([one, total - one])
    tallies = jnp.asarray(split_up(amount, total, limit, skew), jnp.int32)
    pairs = (amount - 1) // 2
    giver, taker = tallies[1:1 + 2 * pairs:2], tallies[2:2 + 2 * pairs:2]
    slack = jnp.minimum(giver - 1, limit - taker)
    passed = jax.random.randint(jax.random.fold_in(own_key, 1), (pairs,), 0, 1 << 20) % (slack + 1)
    tallies = tallies.at[1:1 + 2 * pairs:2].set(giver - passed).at[2:2 + 2 * pairs:2].set(taker + passed)
    return tallies[jax.random.permutation(jax.random.fold_in(own_key, 2), amount)]


def scatter_about(stream_key, dims, scale, most, split=(), held_as=jnp.bfloat16):
    values = scale * jax.random.normal(stream_key, dims, jnp.float32)
    if split:
        values = values * block_levels(stream_key, dims, split, -0.22, 0.18)
    return jnp.clip(values, -most, most).astype(held_as)


def setup_inputs(seed: int = 0) -> dict:
    key_of = jax.random.split(jax.random.key(seed), 15)
    coarse_latents = scatter_about(key_of[0], (MEMBERS, COARSE, H), 1.0, 6.0, ((0, 16), (1, 16)))
    send_rows = touch_ends(jax.random.randint(key_of[1], (N_DOM, N_DOM, SLOT), 0, C_DEV), jax.random.fold_in(key_of[1], 1), 0, C_DEV - 1).astype(jnp.int32)
    up_index = touch_ends(jax.random.randint(key_of[2], (K_UP, POINTS), 0, N_DOM * SLOT), jax.random.fold_in(key_of[2], 1), 0, (N_DOM * SLOT) - 1).astype(jnp.int32)
    up_weight = jnp.clip(0.2 + 0.8 * jax.random.uniform(key_of[3], (K_UP, POINTS), jnp.float32) ** block_levels(key_of[3], (K_UP, POINTS), ((1, 16),), -0.2, 0.2), 0.2, 1.0)
    neighbors = draw_neighbors(jax.random.fold_in(key_of[14], 71), 0)
    live_counts = ragged_sizes(key_of[5], N_DOM, N_DOM * FINE_DEV * 3 // 4, FINE_DEV, 1).astype(jnp.int32)
    area = draw_area(jax.random.fold_in(key_of[14], 71), 0)
    fine_skip = scatter_about(key_of[7], (POINTS, H), 1.0, 6.0, ((0, 16),))
    targets = scatter_about(key_of[8], (VARS, POINTS), 1.0, 6.0, ((1, 16),))
    kernel_width = jnp.clip(jnp.exp(jax.random.uniform(key_of[9], (VARS,), jnp.float32, math.log(0.5), math.log(2.0))), 0.5, 2.0)
    w_in = scatter_about(key_of[10], (2 * H, HID), (2 * H) ** -0.5, 0.1875)
    w_out = scatter_about(key_of[11], (HID, H), HID ** -0.5, 0.25)
    ln_gain = jnp.clip(1.0 + 0.18 * jax.random.normal(key_of[12], (H,), jnp.float32), 0.1, 1.9)
    w_head = scatter_about(key_of[13], (H, VARS), H ** -0.5, 0.25)
    return {"coarse_latents": coarse_latents, "send_rows": send_rows, "up_index": up_index, "up_weight": up_weight, "neighbors": neighbors, "live_counts": live_counts, "area": area, "fine_skip": fine_skip, "targets": targets, "kernel_width": kernel_width, "w_in": w_in, "w_out": w_out, "ln_gain": ln_gain, "w_head": w_head}


def slope(diff, inv_sq):
    return -(diff * inv_sq) * jnp.exp(-0.5 * diff * diff * inv_sq)

def member_pass(coarse_m, send_rows, up_index, up_weight, neighbors, fine_skip, w_in, w_out, ln_gain, w_head):
    blocks = coarse_m.reshape(N_DOM, C_DEV, H)
    sent = jax.vmap(lambda blk, rows: blk[rows])(blocks, send_rows)
    received = jnp.transpose(sent, (1, 0, 2, 3)).reshape(N_DOM, N_DOM * SLOT, H)
    index_blk = up_index.reshape(K_UP, N_DOM, FINE_DEV)
    weight_blk = up_weight.reshape(K_UP, N_DOM, FINE_DEV)
    unpooled = jnp.zeros((N_DOM, FINE_DEV, H), jnp.float32)
    for k in range(K_UP):
        picked = jax.vmap(lambda table, rows: table[rows])(received, index_blk[k])
        unpooled = unpooled + weight_blk[k][:, :, None] * picked.astype(jnp.float32)
    x = (fine_skip.reshape(N_DOM, FINE_DEV, H).astype(jnp.float32) + unpooled).astype(jnp.bfloat16)
    zero_rim = jnp.zeros((1, RIM, H), jnp.bfloat16)
    before = jnp.concatenate([zero_rim, x[:-1, FINE_DEV - RIM:]], axis=0)
    after = jnp.concatenate([x[1:, :RIM], zero_rim], axis=0)
    extended = jnp.concatenate([before, x, after], axis=1)
    nb_blk = neighbors.reshape(K_NB, N_DOM, FINE_DEV)
    total = jnp.zeros((N_DOM, FINE_DEV, H), jnp.float32)
    for k in range(K_NB):
        total = total + jax.vmap(lambda table, rows: table[rows])(extended, nb_blk[k]).astype(jnp.float32)
    agg = (total / K_NB).astype(jnp.bfloat16).reshape(POINTS, H)
    flat_x = x.reshape(POINTS, H)
    pre = jnp.dot(flat_x, w_in[:H], preferred_element_type=jnp.float32) + jnp.dot(agg, w_in[H:], preferred_element_type=jnp.float32)
    act = jax.nn.silu(pre).astype(jnp.bfloat16)
    upd = jnp.dot(act, w_out, preferred_element_type=jnp.float32)
    mean_upd = lax.optimization_barrier(jnp.mean(upd, axis=1, keepdims=True))
    centred = upd - mean_upd
    var_upd = lax.optimization_barrier(jnp.mean(centred * centred, axis=1, keepdims=True))
    hidden = (flat_x.astype(jnp.float32) + centred * lax.rsqrt(var_upd + 1e-05) * ln_gain.astype(jnp.float32)[None, :]).astype(jnp.bfloat16)
    pred = lax.dot_general(w_head, hidden, (((0,), (1,)), ((), ())), preferred_element_type=jnp.float32).astype(jnp.bfloat16)
    return (hidden, pred)

def reference(coarse_latents, send_rows, up_index, up_weight, neighbors, live_counts, area, fine_skip, targets, kernel_width, w_in, w_out, ln_gain, w_head):

    def forward(coarse_m):
        return member_pass(coarse_m, send_rows, up_index, up_weight, neighbors, fine_skip, w_in, w_out, ln_gain, w_head)
    preds = lax.map(lambda c: forward(c)[1], coarse_latents)
    inv_sq = (1.0 / (kernel_width.astype(jnp.float32) * kernel_width.astype(jnp.float32)))[:, None]
    place = jnp.arange(POINTS, dtype=jnp.int32)
    live = (place % FINE_DEV < live_counts[place // FINE_DEV]).astype(jnp.float32)
    weight = (area.astype(jnp.float32) * live)[None, :]
    target_f = targets.astype(jnp.float32)

    def score_one(pred_i):
        pred_f = pred_i.astype(jnp.float32)

        def add_member(j, acc):
            other = lax.dynamic_index_in_dim(preds, j, 0, keepdims=False).astype(jnp.float32)
            return acc + slope(pred_f - other, inv_sq)
        acc = lax.fori_loop(0, MEMBERS, add_member, jnp.zeros((VARS, POINTS), jnp.float32))
        return (weight * (acc / MEMBERS - slope(pred_f - target_f, inv_sq))).astype(jnp.bfloat16)
    gscores = lax.map(score_one, preds)

    def backward(carry, pair):
        coarse_m, gscore = pair
        hidden, unused = forward(coarse_m)
        grad_m = lax.dot_general(gscore, w_head, (((0,), (1,)), ((), ())), preferred_element_type=jnp.float32).astype(jnp.bfloat16)
        hidden_blk = hidden.reshape(N_DOM, FINE_DEV, H).astype(jnp.float32)
        score_blk = gscore.reshape(VARS, N_DOM, FINE_DEV).astype(jnp.float32)
        head_term = jnp.einsum('dph,vdp->dhv', hidden_blk, score_blk)
        return (carry + head_term, grad_m)
    head_total, grad_latent = lax.scan(backward, jnp.zeros((N_DOM, H, VARS), jnp.float32), (coarse_latents, gscores))
    return (grad_latent, head_total * (1.0 / math.sqrt(MEMBERS * FINE_DEV)))
```

```python
import functools
import math

import jax
import jax.numpy as jnp
from jax import lax
from jax.experimental import pallas as pl
from jax.experimental.pallas import tpu as pltpu
from jax.sharding import PartitionSpec as P

F32 = jnp.float32
BF16 = jnp.bfloat16
VARS = 83
VP = 96
NT = (((1,), (1,)), ((), ()))


def lanes_of(row):
    return jnp.broadcast_to(row, (128, 128)).T


def kernel(
    coarse,
    send_rows,
    up_index,
    up_weight,
    neighbors,
    live,
    area,
    skip,
    targets,
    kwidth,
    w_in,
    w_out,
    gain,
    w_head,
    gs_out,
    head_out,
    tiles,
    rows,
    wbuf,
    nbuf,
    cols,
    recv,
    sbuf,
    sibbuf,
    acc,
    skipv,
    ext,
    hidden,
    win,
    wout,
    whp,
    wht,
    kwp,
    inv_b,
    tgt,
    psend,
    pall,
    pf,
    ssend,
    gs,
    hp,
    hr,
    hs,
    hall,
    loc_sem,
    tile_s,
    tile_r,
    rows_s,
    rows_r,
    g_s,
    sib_s,
    recv_sem,
    rim_s,
    rim_r,
    pred_s,
    pred_r,
    gs_s,
    gs_r,
    hr_s,
    hr_r,
    ha_s,
    ha_r,
):
    me_d = lax.axis_index("dom")
    me_m = lax.axis_index("mem")
    c = me_d // 2
    k = me_d - 2 * c
    other = 1 - k

    def chip(offset):
        return lax.rem(c + offset + 8, 8)

    def member(offset):
        return lax.rem(me_m + offset + 16, 16)

    def remote(src, dst, ssem, rsem, **device):
        return pltpu.make_async_remote_copy(
            src_ref=src,
            dst_ref=dst,
            send_sem=ssem,
            recv_sem=rsem,
            device_id=device,
            device_id_type=pl.DeviceIdType.MESH,
        )

    barrier = pltpu.get_barrier_semaphore()

    def greet(r, carry):
        pl.semaphore_signal(
            barrier,
            inc=1,
            device_id={"dom": lax.rem(me_d + r, 16)},
            device_id_type=pl.DeviceIdType.MESH,
        )
        pl.semaphore_signal(
            barrier, inc=1, device_id={"mem": member(r)}, device_id_type=pl.DeviceIdType.MESH
        )
        return carry

    lax.fori_loop(1, 16, greet, 0)
    loads = [
        pltpu.make_async_copy(coarse, tiles.at[0], loc_sem.at[0]),
        pltpu.make_async_copy(skip, skipv, loc_sem.at[1]),
        pltpu.make_async_copy(w_in, win, loc_sem.at[2]),
        pltpu.make_async_copy(w_out, wout, loc_sem.at[3]),
    ]
    for load in loads:
        load.start()
    pl.semaphore_wait(barrier, 30)

    to_right = [
        remote(coarse, tiles.at[1], tile_s.at[0], tile_r.at[0], dom=chip(1) * 2 + k),
        remote(send_rows, rows.at[0], rows_s.at[0], rows_r.at[0], dom=chip(1) * 2 + k),
    ]
    to_left = [
        remote(coarse, tiles.at[2], tile_s.at[1], tile_r.at[1], dom=chip(-1) * 2 + k),
        remote(send_rows, rows.at[1], rows_s.at[1], rows_r.at[1], dom=chip(-1) * 2 + k),
    ]
    for copy in to_right + to_left:
        copy.start()

    lane = lax.broadcasted_iota(jnp.int32, (128, 128), 1).astype(F32)

    def picked(table, tile, dest):
        row = table[pl.ds(dest, 1), :].astype(F32)
        col = lanes_of(row)
        hot = jnp.concatenate(
            [jnp.where(col == lane + 128.0 * q, 1.0, 0.0).astype(BF16) for q in range(4)], axis=1
        )
        return jnp.dot(hot, tile[...], preferred_element_type=F32).astype(BF16)

    my_rows = pl.ds(pl.multiple_of(k * 128, 128), 128)

    def at_home(table, tile, slot, rel):
        sibbuf[slot] = picked(table, tile, me_d + other - k)
        copy = remote(
            sibbuf.at[slot],
            recv.at[rel, my_rows],
            sib_s.at[slot],
            recv_sem.at[rel, k],
            dom=c * 2 + other,
        )
        copy.start()
        recv[rel, my_rows, :] = picked(table, tile, me_d)
        return copy

    loads[0].wait()
    sib_copies = [at_home(send_rows, tiles.at[0], 0, 0)]

    def weights_of(t, carry):
        at = pl.ds(pl.multiple_of(t * 128, 128), 128)
        for j in range(3):
            cols[j] = lanes_of(up_index[j : j + 1, at].astype(F32))
            cols[3 + j] = lanes_of(up_weight[j : j + 1, at])

        def part(s, carry):
            sub = pl.ds(pl.multiple_of(s * 32, 32), 32)
            out = pl.ds(pl.multiple_of(t * 128 + s * 32, 32), 32)
            idx = [cols[j, sub, :] for j in range(3)]
            wgt = [cols[3 + j, sub, :] for j in range(3)]
            base = lax.broadcasted_iota(jnp.int32, (32, 128), 1).astype(F32)
            for q in range(16):
                slot = base + 128.0 * q
                w = (
                    jnp.where(idx[0] == slot, wgt[0], 0.0)
                    + jnp.where(idx[1] == slot, wgt[1], 0.0)
                    + jnp.where(idx[2] == slot, wgt[2], 0.0)
                )
                hi = w.astype(BF16)
                lo = (w - hi.astype(F32)).astype(BF16)
                wbuf[q // 2, out, (q % 2) * 128 : (q % 2) * 128 + 128] = hi
                wbuf[q // 2, out, 256 + (q % 2) * 128 : 384 + (q % 2) * 128] = lo
            return carry

        lax.fori_loop(0, 4, part, 0)
        return carry

    lax.fori_loop(0, 16, weights_of, 0)

    def counts_of(t, carry):
        at = pl.ds(pl.multiple_of(t * 128, 128), 128)
        shift = ((t // 2) * 256).astype(F32)
        for j in range(6):
            cols[j] = lanes_of(neighbors[j : j + 1, at].astype(F32) - shift)

        def part(s, carry):
            sub = pl.ds(pl.multiple_of(s * 32, 32), 32)
            out = pl.ds(pl.multiple_of(t * 128 + s * 32, 32), 32)
            idx = [cols[j, sub, :] for j in range(6)]
            base = lax.broadcasted_iota(jnp.int32, (32, 128), 1).astype(F32)
            for q in range(4):
                spot = base + 128.0 * q
                total = jnp.where(idx[0] == spot, 1.0, 0.0)
                for j in range(1, 6):
                    total = total + jnp.where(idx[j] == spot, 1.0, 0.0)
                nbuf[out, q * 128 : q * 128 + 128] = total.astype(BF16)
            return carry

        lax.fori_loop(0, 4, part, 0)
        return carry

    whp[...] = jnp.zeros((512, 128), F32)
    whp[:, :VARS] = w_head[...].astype(F32)
    for q in range(4):
        wht[:, q * 128 : q * 128 + 128] = whp[q * 128 : q * 128 + 128, :].T[:VP].astype(BF16)
    kwp[...] = jnp.ones((8, 128), F32)
    kwp[0:1, :VARS] = kwidth[...]
    width = kwp[0:1, :]
    inv_b[...] = lanes_of(1.0 / (width * width))[:VP]
    my_share = pl.ds(pl.multiple_of(me_m * 128, 128), 128)
    tgt[...] = jnp.zeros((VP, 128), F32)
    tgt[:VARS, :] = targets[:, my_share].astype(F32)

    lax.fori_loop(0, 16, counts_of, 0)

    for copy in to_right + to_left:
        copy.wait_recv()

    def far_copy(side, j, o, kd):
        dest = chip(o) * 2 + kd
        rel = 4 + (j + 1) // 2 if side == 0 else 4 - (j + 1) // 2
        return dest, remote(
            sbuf.at[side, j],
            recv.at[rel, my_rows],
            g_s.at[side, j],
            recv_sem.at[rel, k],
            dom=dest,
        )

    def both_ways(j, carry):
        o = 3 - (j + 1) // 2
        even = lax.rem(j, 2)
        for side in range(2):
            dest, copy = far_copy(side, j, o if side == 0 else -o, even if side == 0 else 1 - even)
            sbuf[side, j] = picked(rows.at[side], tiles.at[1 + side], dest)
            copy.start()
        return carry

    lax.fori_loop(0, 5, both_ways, 0)
    sib_copies.append(at_home(rows.at[0], tiles.at[1], 1, 7))
    sib_copies.append(at_home(rows.at[1], tiles.at[2], 2, 1))

    loads[1].wait()

    def arrived(rel, kb):
        half = pl.ds(pl.multiple_of(kb * 128, 128), 128)
        remote(
            sibbuf.at[0], recv.at[rel, half], sib_s.at[0], recv_sem.at[rel, kb], dom=c * 2 + other
        ).wait_recv()

    def added(rel, t, first):
        at = pl.ds(pl.multiple_of(t * 256, 256), 256)
        table = recv[rel]
        here = chip(rel)
        total = jnp.dot(wbuf[here, at, :256], table, preferred_element_type=F32)
        total = total + jnp.dot(wbuf[here, at, 256:], table, preferred_element_type=F32)
        before = skipv[at, :].astype(F32) if first else acc[at, :]
        return at, before + total

    for rel in (0, 7, 1, 6, 2, 5, 3):
        arrived(rel, other)
        if rel not in (0, 7, 1):
            arrived(rel, k)

        def accumulate(t, carry, rel=rel):
            at, total = added(rel, t, rel == 0)
            acc[at, :] = total
            return carry

        lax.fori_loop(0, 8, accumulate, 0)

    arrived(4, 0)
    arrived(4, 1)

    def finish(t, carry):
        at, total = added(4, t, False)
        ext[pl.ds(pl.multiple_of(t * 256 + 128, 128), 256), :] = total.astype(BF16)
        return carry

    lax.fori_loop(0, 2, lambda t, carry: finish(t * 7, carry), 0)
    rims = [
        remote(
            ext.at[pl.ds(2048, 128)],
            ext.at[pl.ds(0, 128)],
            rim_s.at[0],
            rim_r.at[0],
            dom=lax.rem(me_d + 1, 16),
        ),
        remote(
            ext.at[pl.ds(128, 128)],
            ext.at[pl.ds(2176, 128)],
            rim_s.at[1],
            rim_r.at[1],
            dom=lax.rem(me_d + 15, 16),
        ),
    ]
    for rim in rims:
        rim.start()
    lax.fori_loop(1, 7, finish, 0)
    loads[2].wait()
    loads[3].wait()

    gain_row = gain[...]

    def pred_copy(j):
        r = lax.rem(j - me_m + 16, 16)
        return r, remote(psend.at[j], pall.at[r], pred_s.at[r], pred_r.at[r], mem=j)

    def dense(i, carry):
        at = pl.ds(pl.multiple_of(i * 256 + 128, 128), 256)
        x = ext[at, :]
        total = jnp.dot(
            nbuf[pl.ds(pl.multiple_of(i * 256, 256), 256), :],
            ext[pl.ds(pl.multiple_of(i * 256, 256), 512), :],
            preferred_element_type=F32,
        )
        agg = (total / 6.0).astype(BF16)
        pre = jnp.dot(x, win[:512], preferred_element_type=F32) + jnp.dot(
            agg, win[512:], preferred_element_type=F32
        )
        half = 0.5 * pre
        act = (half + half * jnp.tanh(half)).astype(BF16)
        upd = jnp.dot(act, wout[...], preferred_element_type=F32)
        mean = jnp.sum(upd, axis=1, keepdims=True) * (1.0 / 512)
        centred = upd - mean
        var = jnp.sum(centred * centred, axis=1, keepdims=True) * (1.0 / 512)
        h = (x.astype(F32) + centred * lax.rsqrt(var + 1e-05) * gain_row).astype(BF16)
        hidden[pl.ds(pl.multiple_of(i * 256, 256), 256), :] = h
        pred = lax.dot_general(wht[...], h, NT, preferred_element_type=F32).astype(BF16)
        for s in range(2):
            j = 2 * i + s
            r, copy = pred_copy(j)
            psend[j] = pred[:, s * 128 : s * 128 + 128]

            @pl.when(r != 0)
            def _():
                copy.start()

            @pl.when(r == 0)
            def _():
                pall[0] = psend[j]

        return carry

    lax.fori_loop(1, 7, dense, 0)
    for rim in rims:
        rim.wait()

    @pl.when(me_d == 0)
    def _():
        ext[pl.ds(0, 128), :] = jnp.zeros((128, 512), BF16)

    @pl.when(me_d == 15)
    def _():
        ext[pl.ds(2176, 128), :] = jnp.zeros((128, 512), BF16)

    lax.fori_loop(0, 2, lambda t, carry: dense(t * 7, carry), 0)

    def pred_wait(r, carry):
        remote(psend.at[0], pall.at[r], pred_s.at[r], pred_r.at[r], mem=member(r)).wait_recv()
        return carry

    lax.fori_loop(1, 16, pred_wait, 0)

    def widen(r, carry):
        pf[r] = pall[r].astype(F32)
        return carry

    lax.fori_loop(0, 16, widen, 0)
    place = lax.broadcasted_iota(jnp.int32, (1, 128), 1) + me_m * 128
    weight = jnp.broadcast_to(jnp.where(place < live[0], area[:, my_share], 0.0), (8, 128))

    def scores(q, carry):
        at = pl.ds(pl.multiple_of(q * 8, 8), 8)
        inv = inv_b[at, :]
        halved = -0.5 * inv
        p = [pf[i, at, :] for i in range(16)]
        t = tgt[at, :]
        total = [None] * 16
        for i in range(16):
            for j in range(i):
                e = p[i] - p[j]
                s = e * jnp.exp(e * e * halved)
                total[i] = s if total[i] is None else total[i] + s
                total[j] = -s if total[j] is None else total[j] - s
        scale = weight * inv
        for i in range(16):
            e = p[i] - t
            pf[i, at, :] = scale * (e * jnp.exp(e * e * halved) - total[i] * (1.0 / 16))
        return carry

    lax.fori_loop(0, VP // 8, scores, 0)
    gs[:, my_share] = pf[0].astype(BF16)

    def gs_copy(r):
        return remote(ssend.at[r], gs.at[:, my_share], gs_s.at[r], gs_r.at[r], mem=member(-r))

    def give_back(r, carry):
        ssend[r] = pf[r].astype(BF16)
        gs_copy(r).start()
        return carry

    lax.fori_loop(1, 16, give_back, 0)

    def gs_wait(r, carry):
        share = pl.ds(pl.multiple_of(member(r) * 128, 128), 128)
        remote(ssend.at[r], gs.at[:, share], gs_s.at[r], gs_r.at[r], mem=member(r)).wait_recv()
        return carry

    lax.fori_loop(1, 16, gs_wait, 0)

    head = jnp.dot(gs[...], hidden[...], preferred_element_type=F32)
    for j in range(16):
        hp[j] = head[24 * (j // 4) : 24 * (j // 4) + 24, 128 * (j % 4) : 128 * (j % 4) + 128]

    def hr_copy(r):
        return remote(hp.at[member(r)], hr.at[r], hr_s.at[r], hr_r.at[r], mem=member(r))

    def spread(r, carry):
        hr_copy(r).start()
        return carry

    lax.fori_loop(1, 16, spread, 0)
    hr[0] = hp[me_m]
    gs_out[...] = gs[:VARS, :]

    def hr_wait(r, carry):
        hr_copy(r).wait_recv()
        return carry

    lax.fori_loop(1, 16, hr_wait, 0)
    summed = hr[0]
    for r in range(1, 16):
        summed = summed + hr[r]
    summed = summed * (1.0 / math.sqrt(32768))
    hs[...] = summed
    hall[me_m] = summed

    def ha_copy(r, owner):
        return remote(hs, hall.at[owner], ha_s.at[r], ha_r.at[r], mem=member(r))

    def tell(r, carry):
        ha_copy(r, me_m).start()
        return carry

    lax.fori_loop(1, 16, tell, 0)

    def ha_wait(r, carry):
        ha_copy(r, member(-r)).wait_recv()
        return carry

    lax.fori_loop(1, 16, ha_wait, 0)
    for j in range(16):
        lo = 24 * (j // 4)
        n = min(24, VARS - lo)
        head_out[lo : lo + n, 128 * (j % 4) : 128 * (j % 4) + 128] = hall[j, :n]

    for copy in to_right + to_left + sib_copies:
        copy.wait_send()

    def far_done(j, carry):
        o = 3 - (j + 1) // 2
        even = lax.rem(j, 2)
        for side in range(2):
            far_copy(side, j, o if side == 0 else -o, even if side == 0 else 1 - even)[
                1
            ].wait_send()
        return carry

    lax.fori_loop(0, 5, far_done, 0)

    def members_done(r, carry):
        pred_copy(member(r))[1].wait_send()
        gs_copy(r).wait_send()
        hr_copy(r).wait_send()
        ha_copy(r, me_m).wait_send()
        return carry

    lax.fori_loop(1, 16, members_done, 0)


def shards(
    coarse_latents,
    send_rows,
    up_index,
    up_weight,
    neighbors,
    live_counts,
    area,
    fine_skip,
    targets,
    kernel_width,
    w_in,
    w_out,
    ln_gain,
    w_head,
):
    hbm = pl.BlockSpec(memory_space=pl.ANY)
    vmem = pl.BlockSpec(memory_space=pltpu.VMEM)
    smem = pl.BlockSpec(memory_space=pltpu.SMEM)
    dma = pltpu.SemaphoreType.DMA
    gscore, head = pl.pallas_call(
        kernel,
        name="decoder_tail",
        out_shape=(
            jax.ShapeDtypeStruct((VARS, 2048), BF16),
            jax.ShapeDtypeStruct((VARS, 512), F32),
        ),
        in_specs=[hbm, vmem, vmem, vmem, vmem, smem, vmem, hbm, vmem, vmem, hbm, hbm, vmem, vmem],
        out_specs=(vmem, vmem),
        scratch_shapes=[
            pltpu.VMEM((3, 512, 512), BF16),
            pltpu.VMEM((2, 16, 128), jnp.int32),
            pltpu.VMEM((8, 2048, 512), BF16),
            pltpu.VMEM((2048, 512), BF16),
            pltpu.VMEM((6, 128, 128), F32),
            pltpu.VMEM((8, 256, 512), BF16),
            pltpu.VMEM((2, 5, 128, 512), BF16),
            pltpu.VMEM((3, 128, 512), BF16),
            pltpu.VMEM((2048, 512), F32),
            pltpu.VMEM((2048, 512), BF16),
            pltpu.VMEM((2304, 512), BF16),
            pltpu.VMEM((2048, 512), BF16),
            pltpu.VMEM((1024, 512), BF16),
            pltpu.VMEM((512, 512), BF16),
            pltpu.VMEM((512, 128), F32),
            pltpu.VMEM((VP, 512), BF16),
            pltpu.VMEM((8, 128), F32),
            pltpu.VMEM((VP, 128), F32),
            pltpu.VMEM((VP, 128), F32),
            pltpu.VMEM((16, VP, 128), BF16),
            pltpu.VMEM((16, VP, 128), BF16),
            pltpu.VMEM((16, VP, 128), F32),
            pltpu.VMEM((16, VP, 128), BF16),
            pltpu.VMEM((VP, 2048), BF16),
            pltpu.VMEM((16, 24, 128), F32),
            pltpu.VMEM((16, 24, 128), F32),
            pltpu.VMEM((24, 128), F32),
            pltpu.VMEM((16, 24, 128), F32),
            dma((4,)),
            dma((2,)),
            dma((2,)),
            dma((2,)),
            dma((2,)),
            dma((2, 5)),
            dma((3,)),
            dma((8, 2)),
            dma((2,)),
            dma((2,)),
            dma((16,)),
            dma((16,)),
            dma((16,)),
            dma((16,)),
            dma((16,)),
            dma((16,)),
            dma((16,)),
            dma((16,)),
        ],
        compiler_params=pltpu.CompilerParams(
            collective_id=0, has_side_effects=True, vmem_limit_bytes=60 * 1024 * 1024
        ),
    )(
        coarse_latents[0],
        send_rows[0],
        up_index,
        up_weight,
        neighbors,
        live_counts,
        area[None],
        fine_skip,
        targets,
        kernel_width[None],
        w_in,
        w_out,
        ln_gain[None],
        w_head,
    )
    grad_latent = lax.dot_general(
        gscore, w_head, (((0,), (1,)), ((), ())), preferred_element_type=F32
    ).astype(BF16)
    return grad_latent[None], head.T[None]


def solution(mesh):
    in_specs = (
        P("mem", "dom", None),
        P("dom", None, None),
        P(None, "dom"),
        P(None, "dom"),
        P(None, "dom"),
        P("dom"),
        P("dom"),
        P("dom", None),
        P(None, "dom"),
        P(),
        P(),
        P(),
        P(),
        P(),
    )
    out_specs = (P("mem", "dom", None), P("dom", None, None))
    return jax.shard_map(
        shards, mesh=mesh, in_specs=in_specs, out_specs=out_specs, check_vma=False
    )
```

```python
import functools
import math

import jax
import jax.numpy as jnp
from jax import lax
from jax.experimental import pallas as pl
from jax.experimental.pallas import tpu as pltpu
from jax.sharding import PartitionSpec as P

F32 = jnp.float32
BF16 = jnp.bfloat16
VARS = 83
VP = 96
NT = (((1,), (1,)), ((), ()))


def lanes_of(row):
    return jnp.broadcast_to(row, (128, 128)).T


def kernel(
    coarse,
    send_rows,
    up_index,
    up_weight,
    neighbors,
    live,
    area,
    skip,
    targets,
    kwidth,
    w_in,
    w_out,
    gain,
    w_head,
    gs_out,
    head_out,
    tiles,
    rows,
    wbuf,
    nbuf,
    cols,
    recv,
    sbuf,
    sibbuf,
    acc,
    skipv,
    ext,
    hidden,
    win,
    wout,
    wht,
    kwp,
    inv_b,
    tgt,
    psend,
    pall,
    pf,
    ssend,
    gs,
    gst,
    hp,
    hr,
    hs,
    hall,
    loc_sem,
    tile_s,
    tile_r,
    rows_s,
    rows_r,
    g_s,
    sib_s,
    recv_sem,
    rim_s,
    rim_r,
    pred_s,
    pred_r,
    gs_s,
    gs_r,
    hr_s,
    hr_r,
    ha_s,
    ha_r,
):
    me_d = lax.axis_index("dom")
    me_m = lax.axis_index("mem")
    c = me_d // 2
    k = me_d - 2 * c
    other = 1 - k

    def chip(offset):
        return lax.rem(c + offset + 8, 8)

    def member(offset):
        return lax.rem(me_m + offset + 16, 16)

    def remote(src, dst, ssem, rsem, **device):
        return pltpu.make_async_remote_copy(
            src_ref=src,
            dst_ref=dst,
            send_sem=ssem,
            recv_sem=rsem,
            device_id=device,
            device_id_type=pl.DeviceIdType.MESH,
        )

    barrier = pltpu.get_barrier_semaphore()

    def greet(r, carry):
        pl.semaphore_signal(
            barrier,
            inc=1,
            device_id={"dom": lax.rem(me_d + r, 16)},
            device_id_type=pl.DeviceIdType.MESH,
        )
        pl.semaphore_signal(
            barrier, inc=1, device_id={"mem": member(r)}, device_id_type=pl.DeviceIdType.MESH
        )
        return carry

    lax.fori_loop(1, 16, greet, 0)
    loads = [
        pltpu.make_async_copy(coarse, tiles.at[0], loc_sem.at[0]),
        pltpu.make_async_copy(skip, skipv, loc_sem.at[1]),
        pltpu.make_async_copy(w_in, win, loc_sem.at[2]),
        pltpu.make_async_copy(w_out, wout, loc_sem.at[3]),
    ]
    for load in loads:
        load.start()
    pl.semaphore_wait(barrier, 30)

    to_right = [
        remote(coarse, tiles.at[1], tile_s.at[0], tile_r.at[0], dom=chip(1) * 2 + k),
        remote(send_rows, rows.at[0], rows_s.at[0], rows_r.at[0], dom=chip(1) * 2 + k),
    ]
    to_left = [
        remote(coarse, tiles.at[2], tile_s.at[1], tile_r.at[1], dom=chip(-1) * 2 + k),
        remote(send_rows, rows.at[1], rows_s.at[1], rows_r.at[1], dom=chip(-1) * 2 + k),
    ]
    for copy in to_right + to_left:
        copy.start()

    lane = lax.broadcasted_iota(jnp.int32, (128, 128), 1).astype(F32)

    def picked(table, tile, dest):
        row = table[pl.ds(dest, 1), :].astype(F32)
        col = lanes_of(row)
        hot = jnp.concatenate(
            [jnp.where(col == lane + 128.0 * q, 1.0, 0.0).astype(BF16) for q in range(4)], axis=1
        )
        return jnp.dot(hot, tile[...], preferred_element_type=F32).astype(BF16)

    my_rows = pl.ds(pl.multiple_of(k * 128, 128), 128)

    def at_home(table, tile, slot, rel):
        sibbuf[slot] = picked(table, tile, me_d + other - k)
        copy = remote(
            sibbuf.at[slot],
            recv.at[rel, my_rows],
            sib_s.at[slot],
            recv_sem.at[rel, k],
            dom=c * 2 + other,
        )
        copy.start()
        recv[rel, my_rows, :] = picked(table, tile, me_d)
        return copy

    loads[0].wait()
    sib_copies = [at_home(send_rows, tiles.at[0], 0, 0)]

    def weights_of(t, carry):
        at = pl.ds(pl.multiple_of(t * 128, 128), 128)
        for j in range(3):
            cols[j] = lanes_of(up_index[j : j + 1, at].astype(F32))
            cols[3 + j] = lanes_of(up_weight[j : j + 1, at])

        def part(s, carry):
            sub = pl.ds(pl.multiple_of(s * 32, 32), 32)
            out = pl.ds(pl.multiple_of(t * 128 + s * 32, 32), 32)
            idx = [cols[j, sub, :] for j in range(3)]
            wgt = [cols[3 + j, sub, :] for j in range(3)]
            base = lax.broadcasted_iota(jnp.int32, (32, 128), 1).astype(F32)
            for q in range(16):
                slot = base + 128.0 * q
                w = (
                    jnp.where(idx[0] == slot, wgt[0], 0.0)
                    + jnp.where(idx[1] == slot, wgt[1], 0.0)
                    + jnp.where(idx[2] == slot, wgt[2], 0.0)
                )
                hi = w.astype(BF16)
                lo = (w - hi.astype(F32)).astype(BF16)
                wbuf[q // 2, out, (q % 2) * 128 : (q % 2) * 128 + 128] = hi
                wbuf[q // 2, out, 256 + (q % 2) * 128 : 384 + (q % 2) * 128] = lo
            return carry

        lax.fori_loop(0, 4, part, 0)
        return carry

    lax.fori_loop(0, 16, weights_of, 0)

    def counts_of(t, carry):
        at = pl.ds(pl.multiple_of(t * 128, 128), 128)
        shift = ((t // 2) * 256).astype(F32)
        for j in range(6):
            cols[j] = lanes_of(neighbors[j : j + 1, at].astype(F32) - shift)

        def part(s, carry):
            sub = pl.ds(pl.multiple_of(s * 32, 32), 32)
            out = pl.ds(pl.multiple_of(t * 128 + s * 32, 32), 32)
            idx = [cols[j, sub, :] for j in range(6)]
            base = lax.broadcasted_iota(jnp.int32, (32, 128), 1).astype(F32)
            for q in range(4):
                spot = base + 128.0 * q
                total = jnp.where(idx[0] == spot, 1.0, 0.0)
                for j in range(1, 6):
                    total = total + jnp.where(idx[j] == spot, 1.0, 0.0)
                nbuf[out, q * 128 : q * 128 + 128] = total.astype(BF16)
            return carry

        lax.fori_loop(0, 4, part, 0)
        return carry

    wht[...] = jnp.zeros((VP, 512), BF16)
    wht[:VARS, :] = w_head[...]
    kwp[...] = jnp.ones((8, 128), F32)
    kwp[0:1, :VARS] = kwidth[...]
    width = kwp[0:1, :]
    inv_b[...] = lanes_of(1.0 / (width * width))[:VP]
    my_share = pl.ds(pl.multiple_of(me_m * 128, 128), 128)
    tgt[...] = jnp.zeros((VP, 128), F32)
    tgt[:VARS, :] = targets[:, my_share].astype(F32)

    lax.fori_loop(0, 16, counts_of, 0)

    for copy in to_right + to_left:
        copy.wait_recv()

    def far_copy(side, j, o, kd):
        dest = chip(o) * 2 + kd
        rel = 4 + (j + 1) // 2 if side == 0 else 4 - (j + 1) // 2
        return dest, remote(
            sbuf.at[side, j],
            recv.at[rel, my_rows],
            g_s.at[side, j],
            recv_sem.at[rel, k],
            dom=dest,
        )

    def both_ways(j, carry):
        o = 3 - (j + 1) // 2
        even = lax.rem(j, 2)
        for side in range(2):
            dest, copy = far_copy(side, j, o if side == 0 else -o, even if side == 0 else 1 - even)
            sbuf[side, j] = picked(rows.at[side], tiles.at[1 + side], dest)
            copy.start()
        return carry

    lax.fori_loop(0, 5, both_ways, 0)
    sib_copies.append(at_home(rows.at[0], tiles.at[1], 1, 7))
    sib_copies.append(at_home(rows.at[1], tiles.at[2], 2, 1))

    loads[1].wait()

    def arrived(rel, kb):
        half = pl.ds(pl.multiple_of(kb * 128, 128), 128)
        remote(
            sibbuf.at[0], recv.at[rel, half], sib_s.at[0], recv_sem.at[rel, kb], dom=c * 2 + other
        ).wait_recv()

    def added(rels, t):
        at = pl.ds(pl.multiple_of(t * 512, 512), 512)
        total = skipv[at, :].astype(F32) if rels == (0,) else acc[at, :]
        for rel in rels:
            here = chip(rel)
            table = recv[rel]
            total = total + jnp.dot(wbuf[here, at, :256], table, preferred_element_type=F32)
            total = total + jnp.dot(wbuf[here, at, 256:], table, preferred_element_type=F32)
        return at, total

    for rels in ((0,), (7, 1), (4,), (5, 3)):
        for rel in rels:
            arrived(rel, other)
            if rel not in (0, 7, 1):
                arrived(rel, k)

        def accumulate(t, carry, rels=rels):
            at, total = added(rels, t)
            acc[at, :] = total
            return carry

        lax.fori_loop(0, 4, accumulate, 0)

    for rel in (6, 2):
        arrived(rel, 0)
        arrived(rel, 1)

    def finish(t, carry):
        total = added((6, 2), t)[1]
        ext[pl.ds(pl.multiple_of(t * 512 + 128, 128), 512), :] = total.astype(BF16)
        return carry

    lax.fori_loop(0, 2, lambda t, carry: finish(t * 3, carry), 0)
    rims = [
        remote(
            ext.at[pl.ds(2048, 128)],
            ext.at[pl.ds(0, 128)],
            rim_s.at[0],
            rim_r.at[0],
            dom=lax.rem(me_d + 1, 16),
        ),
        remote(
            ext.at[pl.ds(128, 128)],
            ext.at[pl.ds(2176, 128)],
            rim_s.at[1],
            rim_r.at[1],
            dom=lax.rem(me_d + 15, 16),
        ),
    ]
    for rim in rims:
        rim.start()
    lax.fori_loop(1, 3, finish, 0)
    loads[2].wait()
    loads[3].wait()

    gain_row = gain[...]

    def pred_copy(j):
        r = lax.rem(j - me_m + 16, 16)
        return r, remote(psend.at[j], pall.at[r], pred_s.at[r], pred_r.at[r], mem=j)

    def dense(i, carry):
        x = ext[pl.ds(pl.multiple_of(i * 512 + 128, 128), 512), :]
        parts = []
        for s in range(2):
            start = pl.multiple_of(i * 512 + s * 256, 256)
            total = jnp.dot(
                nbuf[pl.ds(start, 256), :], ext[pl.ds(start, 512), :], preferred_element_type=F32
            )
            parts.append((total * (1.0 / 6)).astype(BF16))
        agg = jnp.concatenate(parts, axis=0)
        pre = jnp.dot(x, win[:512], preferred_element_type=F32) + jnp.dot(
            agg, win[512:], preferred_element_type=F32
        )
        half = 0.5 * pre
        act = (half + half * jnp.tanh(half)).astype(BF16)
        upd = jnp.dot(act, wout[...], preferred_element_type=F32)
        mean = jnp.sum(upd, axis=1, keepdims=True) * (1.0 / 512)
        centred = upd - mean
        var = jnp.sum(centred * centred, axis=1, keepdims=True) * (1.0 / 512)
        h = (x.astype(F32) + centred * lax.rsqrt(var + 1e-05) * gain_row).astype(BF16)
        hidden[pl.ds(pl.multiple_of(i * 512, 512), 512), :] = h
        pred = lax.dot_general(wht[...], h, NT, preferred_element_type=F32).astype(BF16)
        for s in range(4):
            j = 4 * i + s
            r, copy = pred_copy(j)
            psend[j] = pred[:, s * 128 : s * 128 + 128]

            @pl.when(r != 0)
            def _():
                copy.start()

            @pl.when(r == 0)
            def _():
                pall[0] = psend[j]

        return carry

    lax.fori_loop(1, 3, dense, 0)
    for rim in rims:
        rim.wait()

    @pl.when(me_d == 0)
    def _():
        ext[pl.ds(0, 128), :] = jnp.zeros((128, 512), BF16)

    @pl.when(me_d == 15)
    def _():
        ext[pl.ds(2176, 128), :] = jnp.zeros((128, 512), BF16)

    lax.fori_loop(0, 2, lambda t, carry: dense(t * 3, carry), 0)

    def pred_wait(r, carry):
        remote(psend.at[0], pall.at[r], pred_s.at[r], pred_r.at[r], mem=member(r)).wait_recv()
        return carry

    lax.fori_loop(1, 16, pred_wait, 0)

    def widen(r, carry):
        pf[r] = pall[r].astype(F32)
        return carry

    lax.fori_loop(0, 16, widen, 0)
    place = lax.broadcasted_iota(jnp.int32, (1, 128), 1) + me_m * 128
    weight = jnp.broadcast_to(jnp.where(place < live[0], area[:, my_share], 0.0), (8, 128))

    def scores(q, carry):
        at = pl.ds(pl.multiple_of(q * 8, 8), 8)
        inv = inv_b[at, :]
        halved = -0.5 * inv
        p = [pf[i, at, :] for i in range(16)]
        t = tgt[at, :]
        total = [None] * 16
        for i in range(16):
            for j in range(i):
                e = p[i] - p[j]
                s = e * jnp.exp(e * e * halved)
                total[i] = s if total[i] is None else total[i] + s
                total[j] = -s if total[j] is None else total[j] - s
        scale = weight * inv
        for i in range(16):
            e = p[i] - t
            pf[i, at, :] = scale * (e * jnp.exp(e * e * halved) - total[i] * (1.0 / 16))
        return carry

    lax.fori_loop(0, VP // 8, scores, 0)
    gs[:, my_share] = pf[0].astype(BF16)

    def gs_copy(r):
        return remote(ssend.at[r], gs.at[:, my_share], gs_s.at[r], gs_r.at[r], mem=member(-r))

    def give_back(r, carry):
        ssend[r] = pf[r].astype(BF16)
        gs_copy(r).start()
        return carry

    lax.fori_loop(1, 16, give_back, 0)

    def gs_wait(r, carry):
        share = pl.ds(pl.multiple_of(member(r) * 128, 128), 128)
        remote(ssend.at[r], gs.at[:, share], gs_s.at[r], gs_r.at[r], mem=member(r)).wait_recv()
        return carry

    lax.fori_loop(1, 16, gs_wait, 0)

    head = jnp.dot(gs[...], hidden[...], preferred_element_type=F32)
    for j in range(16):
        hp[j] = head[24 * (j // 4) : 24 * (j // 4) + 24, 128 * (j % 4) : 128 * (j % 4) + 128]

    def hr_copy(r):
        return remote(hp.at[member(r)], hr.at[r], hr_s.at[r], hr_r.at[r], mem=member(r))

    def spread(r, carry):
        hr_copy(r).start()
        return carry

    lax.fori_loop(1, 16, spread, 0)
    hr[0] = hp[me_m]

    def turn(j, carry):
        at = pl.ds(pl.multiple_of(j * 128, 128), 128)
        gst[at, :] = gs[:, at].astype(F32).T[:, :VARS].astype(BF16)
        return carry

    lax.fori_loop(0, 16, turn, 0)
    turned = pltpu.make_async_copy(gst, gs_out, loc_sem.at[4])
    turned.start()

    def hr_wait(r, carry):
        hr_copy(r).wait_recv()
        return carry

    lax.fori_loop(1, 16, hr_wait, 0)
    summed = hr[0]
    for r in range(1, 16):
        summed = summed + hr[r]
    summed = summed * (1.0 / math.sqrt(32768))
    hs[...] = summed
    hall[me_m] = summed

    def ha_copy(r, owner):
        return remote(hs, hall.at[owner], ha_s.at[r], ha_r.at[r], mem=member(r))

    def tell(r, carry):
        ha_copy(r, me_m).start()
        return carry

    lax.fori_loop(1, 16, tell, 0)

    def ha_wait(r, carry):
        ha_copy(r, member(-r)).wait_recv()
        return carry

    lax.fori_loop(1, 16, ha_wait, 0)
    for j in range(16):
        lo = 24 * (j // 4)
        n = min(24, VARS - lo)
        head_out[lo : lo + n, 0, 128 * (j % 4) : 128 * (j % 4) + 128] = hall[j, :n]

    turned.wait()
    for copy in to_right + to_left + sib_copies:
        copy.wait_send()

    def far_done(j, carry):
        o = 3 - (j + 1) // 2
        even = lax.rem(j, 2)
        for side in range(2):
            far_copy(side, j, o if side == 0 else -o, even if side == 0 else 1 - even)[
                1
            ].wait_send()
        return carry

    lax.fori_loop(0, 5, far_done, 0)

    def members_done(r, carry):
        pred_copy(member(r))[1].wait_send()
        gs_copy(r).wait_send()
        hr_copy(r).wait_send()
        ha_copy(r, me_m).wait_send()
        return carry

    lax.fori_loop(1, 16, members_done, 0)


def shards(
    coarse_latents,
    send_rows,
    up_index,
    up_weight,
    neighbors,
    live_counts,
    area,
    fine_skip,
    targets,
    kernel_width,
    w_in,
    w_out,
    ln_gain,
    w_head,
):
    hbm = pl.BlockSpec(memory_space=pl.ANY)
    vmem = pl.BlockSpec(memory_space=pltpu.VMEM)
    smem = pl.BlockSpec(memory_space=pltpu.SMEM)
    dma = pltpu.SemaphoreType.DMA
    gscore, head = pl.pallas_call(
        kernel,
        name="decoder_tail",
        out_shape=(
            jax.ShapeDtypeStruct((2048, VARS), BF16),
            jax.ShapeDtypeStruct((VARS, 1, 512), F32),
        ),
        in_specs=[hbm, vmem, vmem, vmem, vmem, smem, vmem, hbm, vmem, vmem, hbm, hbm, vmem, vmem],
        out_specs=(hbm, vmem),
        scratch_shapes=[
            pltpu.VMEM((3, 512, 512), BF16),
            pltpu.VMEM((2, 16, 128), jnp.int32),
            pltpu.VMEM((8, 2048, 512), BF16),
            pltpu.VMEM((2048, 512), BF16),
            pltpu.VMEM((6, 128, 128), F32),
            pltpu.VMEM((8, 256, 512), BF16),
            pltpu.VMEM((2, 5, 128, 512), BF16),
            pltpu.VMEM((3, 128, 512), BF16),
            pltpu.VMEM((2048, 512), F32),
            pltpu.VMEM((2048, 512), BF16),
            pltpu.VMEM((2304, 512), BF16),
            pltpu.VMEM((2048, 512), BF16),
            pltpu.VMEM((1024, 512), BF16),
            pltpu.VMEM((512, 512), BF16),
            pltpu.VMEM((VP, 512), BF16),
            pltpu.VMEM((8, 128), F32),
            pltpu.VMEM((VP, 128), F32),
            pltpu.VMEM((VP, 128), F32),
            pltpu.VMEM((16, VP, 128), BF16),
            pltpu.VMEM((16, VP, 128), BF16),
            pltpu.VMEM((16, VP, 128), F32),
            pltpu.VMEM((16, VP, 128), BF16),
            pltpu.VMEM((VP, 2048), BF16),
            pltpu.VMEM((2048, VARS), BF16),
            pltpu.VMEM((16, 24, 128), F32),
            pltpu.VMEM((16, 24, 128), F32),
            pltpu.VMEM((24, 128), F32),
            pltpu.VMEM((16, 24, 128), F32),
            dma((5,)),
            dma((2,)),
            dma((2,)),
            dma((2,)),
            dma((2,)),
            dma((2, 5)),
            dma((3,)),
            dma((8, 2)),
            dma((2,)),
            dma((2,)),
            dma((16,)),
            dma((16,)),
            dma((16,)),
            dma((16,)),
            dma((16,)),
            dma((16,)),
            dma((16,)),
            dma((16,)),
        ],
        compiler_params=pltpu.CompilerParams(
            collective_id=0, has_side_effects=True, vmem_limit_bytes=60 * 1024 * 1024
        ),
    )(
        coarse_latents[0],
        send_rows[0],
        up_index,
        up_weight,
        neighbors,
        live_counts,
        area[None],
        fine_skip,
        targets,
        kernel_width[None],
        w_in,
        w_out,
        ln_gain[None],
        w_head.T,
    )
    grad_latent = lax.dot_general(
        gscore, w_head, (((1,), (1,)), ((), ())), preferred_element_type=F32
    ).astype(BF16)
    return grad_latent[None], head.transpose(1, 2, 0)


def solution(mesh):
    in_specs = (
        P("mem", "dom", None),
        P("dom", None, None),
        P(None, "dom"),
        P(None, "dom"),
        P(None, "dom"),
        P("dom"),
        P("dom"),
        P("dom", None),
        P(None, "dom"),
        P(),
        P(),
        P(),
        P(),
        P(),
    )
    out_specs = (P("mem", "dom", None), P("dom", None, None))
    return jax.shard_map(
        shards, mesh=mesh, in_specs=in_specs, out_specs=out_specs, check_vma=False
    )
```

```python
import functools
import math

import jax
import jax.numpy as jnp
from jax import lax
from jax.experimental import pallas as pl
from jax.experimental.pallas import tpu as pltpu
from jax.sharding import PartitionSpec as P

F32 = jnp.float32
BF16 = jnp.bfloat16
VARS = 83
VP = 96
NT = (((1,), (1,)), ((), ()))


def lanes_of(row):
    return jnp.broadcast_to(row, (128, 128)).T


def kernel(
    coarse,
    send_rows,
    up_index,
    up_weight,
    neighbors,
    live,
    area,
    skip,
    targets,
    kwidth,
    w_in,
    w_out,
    gain,
    w_head,
    gs_out,
    head_out,
    tiles,
    rows,
    wbuf,
    nbuf,
    cols,
    recv,
    sbuf,
    sibbuf,
    acc,
    part,
    skipv,
    ext,
    hidden,
    win,
    wout,
    wht,
    kwp,
    inv_b,
    tgt,
    psend,
    pall,
    pf,
    ssend,
    gs,
    gst,
    hp,
    hr,
    hs,
    hall,
    loc_sem,
    tile_s,
    tile_r,
    rows_s,
    rows_r,
    g_s,
    sib_s,
    recv_sem,
    rim_s,
    rim_r,
    pred_s,
    pred_r,
    gs_s,
    gs_r,
    hr_s,
    hr_r,
    ha_s,
    ha_r,
):
    me_d = lax.axis_index("dom")
    me_m = lax.axis_index("mem")
    c = me_d // 2
    k = me_d - 2 * c
    other = 1 - k

    def chip(offset):
        return lax.rem(c + offset + 8, 8)

    def member(offset):
        return lax.rem(me_m + offset + 16, 16)

    def remote(src, dst, ssem, rsem, **device):
        return pltpu.make_async_remote_copy(
            src_ref=src,
            dst_ref=dst,
            send_sem=ssem,
            recv_sem=rsem,
            device_id=device,
            device_id_type=pl.DeviceIdType.MESH,
        )

    barrier = pltpu.get_barrier_semaphore()

    def greet(r, carry):
        pl.semaphore_signal(
            barrier,
            inc=1,
            device_id={"dom": lax.rem(me_d + r, 16)},
            device_id_type=pl.DeviceIdType.MESH,
        )
        pl.semaphore_signal(
            barrier, inc=1, device_id={"mem": member(r)}, device_id_type=pl.DeviceIdType.MESH
        )
        return carry

    lax.fori_loop(1, 16, greet, 0)
    loads = [
        pltpu.make_async_copy(coarse.at[:, :256], tiles.at[0, 0], loc_sem.at[0]),
        pltpu.make_async_copy(skip, skipv, loc_sem.at[1]),
        pltpu.make_async_copy(w_in, win, loc_sem.at[2]),
        pltpu.make_async_copy(w_out, wout, loc_sem.at[3]),
        pltpu.make_async_copy(coarse.at[:, 256:], tiles.at[1, 0], loc_sem.at[4]),
    ]
    for load in loads:
        load.start()
    pl.semaphore_wait(barrier, 30)

    next_to = (chip(1) * 2 + k, chip(-1) * 2 + k)
    row_copies = [
        remote(send_rows, rows.at[i], rows_s.at[i], rows_r.at[i], dom=next_to[i]) for i in range(2)
    ]
    tile_copies = [
        [
            remote(
                coarse.at[:, 256 * h : 256 * h + 256],
                tiles.at[h, 1 + i],
                tile_s.at[h, i],
                tile_r.at[h, i],
                dom=next_to[i],
            )
            for i in range(2)
        ]
        for h in range(2)
    ]
    for copy in row_copies + tile_copies[0] + tile_copies[1]:
        copy.start()

    lane = lax.broadcasted_iota(jnp.int32, (128, 128), 1).astype(F32)

    def picked(table, tile, dest):
        row = table[pl.ds(dest, 1), :].astype(F32)
        col = lanes_of(row)
        hot = jnp.concatenate(
            [jnp.where(col == lane + 128.0 * q, 1.0, 0.0).astype(BF16) for q in range(4)], axis=1
        )
        return jnp.dot(hot, tile[...], preferred_element_type=F32).astype(BF16)

    my_rows = pl.ds(pl.multiple_of(k * 128, 128), 128)

    def at_home(h, table, slot, rel):
        tile = tiles.at[h, slot]
        sibbuf[h, slot] = picked(table, tile, me_d + other - k)
        copy = remote(
            sibbuf.at[h, slot],
            recv.at[h, rel, my_rows],
            sib_s.at[h, slot],
            recv_sem.at[h, rel, k],
            dom=c * 2 + other,
        )
        copy.start()
        recv[h, rel, my_rows, :] = picked(table, tile, me_d)
        return copy

    loads[0].wait()
    loads[4].wait()
    sib_copies = [at_home(0, send_rows, 0, 0), at_home(1, send_rows, 0, 0)]

    def weights_of(t, carry):
        at = pl.ds(pl.multiple_of(t * 128, 128), 128)
        for j in range(3):
            cols[j] = lanes_of(up_index[j : j + 1, at].astype(F32))
            cols[3 + j] = lanes_of(up_weight[j : j + 1, at])

        def rows_of(s, carry):
            sub = pl.ds(pl.multiple_of(s * 32, 32), 32)
            out = pl.ds(pl.multiple_of(t * 128 + s * 32, 32), 32)
            idx = [cols[j, sub, :] for j in range(3)]
            wgt = [cols[3 + j, sub, :] for j in range(3)]
            base = lax.broadcasted_iota(jnp.int32, (32, 128), 1).astype(F32)
            for q in range(16):
                slot = base + 128.0 * q
                w = (
                    jnp.where(idx[0] == slot, wgt[0], 0.0)
                    + jnp.where(idx[1] == slot, wgt[1], 0.0)
                    + jnp.where(idx[2] == slot, wgt[2], 0.0)
                )
                hi = w.astype(BF16)
                lo = (w - hi.astype(F32)).astype(BF16)
                wbuf[q // 2, out, (q % 2) * 128 : (q % 2) * 128 + 128] = hi
                wbuf[q // 2, out, 256 + (q % 2) * 128 : 384 + (q % 2) * 128] = lo
            return carry

        lax.fori_loop(0, 4, rows_of, 0)
        return carry

    def counts_of(t, carry):
        at = pl.ds(pl.multiple_of(t * 128, 128), 128)
        shift = ((t // 2) * 256).astype(F32)
        for j in range(6):
            cols[j] = lanes_of(neighbors[j : j + 1, at].astype(F32) - shift)

        def rows_of(s, carry):
            sub = pl.ds(pl.multiple_of(s * 32, 32), 32)
            out = pl.ds(pl.multiple_of(t * 128 + s * 32, 32), 32)
            idx = [cols[j, sub, :] for j in range(6)]
            base = lax.broadcasted_iota(jnp.int32, (32, 128), 1).astype(F32)
            for q in range(4):
                spot = base + 128.0 * q
                total = jnp.where(idx[0] == spot, 1.0, 0.0)
                for j in range(1, 6):
                    total = total + jnp.where(idx[j] == spot, 1.0, 0.0)
                nbuf[out, q * 128 : q * 128 + 128] = total.astype(BF16)
            return carry

        lax.fori_loop(0, 4, rows_of, 0)
        return carry

    wht[...] = jnp.zeros((VP, 512), BF16)
    wht[:VARS, :] = w_head[...]
    kwp[...] = jnp.ones((8, 128), F32)
    kwp[0:1, :VARS] = kwidth[...]
    width = kwp[0:1, :]
    inv_b[...] = lanes_of(1.0 / (width * width))[:VP]
    my_share = pl.ds(pl.multiple_of(me_m * 128, 128), 128)
    tgt[...] = jnp.zeros((VP, 128), F32)
    tgt[:VARS, :] = targets[:, my_share].astype(F32)

    lax.fori_loop(0, 16, counts_of, 0)

    def far_copy(h, side, j, o, kd):
        dest = chip(o) * 2 + kd
        rel = 4 + (j + 1) // 2 if side == 0 else 4 - (j + 1) // 2
        return dest, remote(
            sbuf.at[h, side, j],
            recv.at[h, rel, my_rows],
            g_s.at[h, side, j],
            recv_sem.at[h, rel, k],
            dom=dest,
        )

    def send_on(h):
        for copy in tile_copies[h]:
            copy.wait_recv()

        def both_ways(j, carry):
            o = 3 - (j + 1) // 2
            even = lax.rem(j, 2)
            for side in range(2):
                dest, copy = far_copy(
                    h, side, j, o if side == 0 else -o, even if side == 0 else 1 - even
                )
                sbuf[h, side, j] = picked(rows.at[side], tiles.at[h, 1 + side], dest)
                copy.start()
            return carry

        lax.fori_loop(0, 5, both_ways, 0)
        sib_copies.append(at_home(h, rows.at[0], 1, 7))
        sib_copies.append(at_home(h, rows.at[1], 2, 1))

    for copy in row_copies:
        copy.wait_recv()
    send_on(0)
    lax.fori_loop(0, 16, weights_of, 0)
    send_on(1)
    for load in loads[1:4]:
        load.wait()

    def arrived(h, rel, kb):
        half = pl.ds(pl.multiple_of(kb * 128, 128), 128)
        remote(
            sibbuf.at[h, 0],
            recv.at[h, rel, half],
            sib_s.at[h, 0],
            recv_sem.at[h, rel, kb],
            dom=c * 2 + other,
        ).wait_recv()

    def unpooled(h):
        mine = slice(256 * h, 256 * h + 256)

        def added(rels, t):
            at = pl.ds(pl.multiple_of(t * 512, 512), 512)
            total = skipv[at, mine].astype(F32) if rels == (0,) else acc[at, :]
            for rel in rels:
                here = chip(rel)
                table = recv[h, rel]
                total = total + jnp.dot(wbuf[here, at, :256], table, preferred_element_type=F32)
                total = total + jnp.dot(wbuf[here, at, 256:], table, preferred_element_type=F32)
            return at, total

        for rels in ((0,), (7, 1), (4,), (5, 3)):
            for rel in rels:
                arrived(h, rel, other)
                if rel not in (0, 7, 1):
                    arrived(h, rel, k)

            def accumulate(t, carry, rels=rels):
                at, total = added(rels, t)
                acc[at, :] = total
                return carry

            lax.fori_loop(0, 4, accumulate, 0)

        for rel in (6, 2):
            arrived(h, rel, 0)
            arrived(h, rel, 1)

        def finish(t, carry):
            total = added((6, 2), t)[1]
            ext[h, pl.ds(pl.multiple_of(t * 512 + 128, 128), 512), :] = total.astype(BF16)
            return carry

        lax.fori_loop(0, 2, lambda t, carry: finish(t * 3, carry), 0)
        rims = [
            remote(
                ext.at[h, pl.ds(2048, 128)],
                ext.at[h, pl.ds(0, 128)],
                rim_s.at[h, 0],
                rim_r.at[h, 0],
                dom=lax.rem(me_d + 1, 16),
            ),
            remote(
                ext.at[h, pl.ds(128, 128)],
                ext.at[h, pl.ds(2176, 128)],
                rim_s.at[h, 1],
                rim_r.at[h, 1],
                dom=lax.rem(me_d + 15, 16),
            ),
        ]
        for rim in rims:
            rim.start()
        lax.fori_loop(1, 3, finish, 0)
        return rims

    def rims_done(h, rims):
        for rim in rims:
            rim.wait()

        @pl.when(me_d == 0)
        def _():
            ext[h, pl.ds(0, 128), :] = jnp.zeros((128, 256), BF16)

        @pl.when(me_d == 15)
        def _():
            ext[h, pl.ds(2176, 128), :] = jnp.zeros((128, 256), BF16)

    def half_pre(h, i):
        x = ext[h, pl.ds(pl.multiple_of(i * 512 + 128, 128), 512), :]
        parts = []
        for s in range(2):
            start = pl.multiple_of(i * 512 + s * 256, 256)
            total = jnp.dot(
                nbuf[pl.ds(start, 256), :],
                ext[h, pl.ds(start, 512), :],
                preferred_element_type=F32,
            )
            parts.append((total * (1.0 / 6)).astype(BF16))
        agg = jnp.concatenate(parts, axis=0)
        lo = 256 * h
        return x, jnp.dot(x, win[lo : lo + 256], preferred_element_type=F32) + jnp.dot(
            agg, win[512 + lo : 768 + lo], preferred_element_type=F32
        )

    def begin(i, carry):
        part[pl.ds(pl.multiple_of(i * 512, 512), 512), :] = half_pre(0, i)[1]
        return carry

    first_rims = unpooled(0)
    lax.fori_loop(1, 3, begin, 0)
    rims_done(0, first_rims)
    lax.fori_loop(0, 2, lambda t, carry: begin(t * 3, carry), 0)
    rims = unpooled(1)

    gain_row = gain[...]

    def pred_copy(j):
        r = lax.rem(j - me_m + 16, 16)
        return r, remote(psend.at[j], pall.at[r], pred_s.at[r], pred_r.at[r], mem=j)

    def dense(i, carry):
        late, pre = half_pre(1, i)
        pre = pre + part[pl.ds(pl.multiple_of(i * 512, 512), 512), :]
        early = ext[0, pl.ds(pl.multiple_of(i * 512 + 128, 128), 512), :]
        x = jnp.concatenate([early, late], axis=1)
        half = 0.5 * pre
        act = (half + half * jnp.tanh(half)).astype(BF16)
        upd = jnp.dot(act, wout[...], preferred_element_type=F32)
        mean = jnp.sum(upd, axis=1, keepdims=True) * (1.0 / 512)
        centred = upd - mean
        var = jnp.sum(centred * centred, axis=1, keepdims=True) * (1.0 / 512)
        h = (x.astype(F32) + centred * lax.rsqrt(var + 1e-05) * gain_row).astype(BF16)
        hidden[pl.ds(pl.multiple_of(i * 512, 512), 512), :] = h
        pred = lax.dot_general(wht[...], h, NT, preferred_element_type=F32).astype(BF16)
        for s in range(4):
            j = 4 * i + s
            r, copy = pred_copy(j)
            psend[j] = pred[:, s * 128 : s * 128 + 128]

            @pl.when(r != 0)
            def _():
                copy.start()

            @pl.when(r == 0)
            def _():
                pall[0] = psend[j]

        return carry

    lax.fori_loop(1, 3, dense, 0)
    rims_done(1, rims)
    lax.fori_loop(0, 2, lambda t, carry: dense(t * 3, carry), 0)

    def pred_wait(r, carry):
        remote(psend.at[0], pall.at[r], pred_s.at[r], pred_r.at[r], mem=member(r)).wait_recv()
        return carry

    lax.fori_loop(1, 16, pred_wait, 0)

    def widen(r, carry):
        pf[r] = pall[r].astype(F32)
        return carry

    lax.fori_loop(0, 16, widen, 0)
    place = lax.broadcasted_iota(jnp.int32, (1, 128), 1) + me_m * 128
    weight = jnp.broadcast_to(jnp.where(place < live[0], area[:, my_share], 0.0), (8, 128))

    def scores(q, carry):
        at = pl.ds(pl.multiple_of(q * 8, 8), 8)
        inv = inv_b[at, :]
        halved = -0.5 * inv
        p = [pf[i, at, :] for i in range(16)]
        t = tgt[at, :]
        total = [None] * 16
        for i in range(16):
            for j in range(i):
                e = p[i] - p[j]
                s = e * jnp.exp(e * e * halved)
                total[i] = s if total[i] is None else total[i] + s
                total[j] = -s if total[j] is None else total[j] - s
        scale = weight * inv
        for i in range(16):
            e = p[i] - t
            pf[i, at, :] = scale * (e * jnp.exp(e * e * halved) - total[i] * (1.0 / 16))
        return carry

    lax.fori_loop(0, VP // 8, scores, 0)
    gs[:, my_share] = pf[0].astype(BF16)

    def gs_copy(r):
        return remote(ssend.at[r], gs.at[:, my_share], gs_s.at[r], gs_r.at[r], mem=member(-r))

    def give_back(r, carry):
        ssend[r] = pf[r].astype(BF16)
        gs_copy(r).start()
        return carry

    lax.fori_loop(1, 16, give_back, 0)

    def gs_wait(r, carry):
        share = pl.ds(pl.multiple_of(member(r) * 128, 128), 128)
        remote(ssend.at[r], gs.at[:, share], gs_s.at[r], gs_r.at[r], mem=member(r)).wait_recv()
        return carry

    lax.fori_loop(1, 16, gs_wait, 0)

    head = jnp.dot(gs[...], hidden[...], preferred_element_type=F32)
    for j in range(16):
        lo, left = 24 * (j // 4), 128 * (j % 4)
        hp[j] = head[lo : lo + 24, left : left + 128].astype(BF16)

    def hr_copy(r):
        return remote(hp.at[member(r)], hr.at[r], hr_s.at[r], hr_r.at[r], mem=member(r))

    def spread(r, carry):
        hr_copy(r).start()
        return carry

    lax.fori_loop(1, 16, spread, 0)
    hr[0] = hp[me_m]

    def turn(j, carry):
        at = pl.ds(pl.multiple_of(j * 128, 128), 128)
        gst[at, :] = gs[:, at].astype(F32).T[:, :VARS].astype(BF16)
        return carry

    lax.fori_loop(0, 16, turn, 0)
    turned = pltpu.make_async_copy(gst, gs_out, loc_sem.at[5])
    turned.start()

    def hr_wait(r, carry):
        hr_copy(r).wait_recv()
        return carry

    lax.fori_loop(1, 16, hr_wait, 0)
    summed = hr[0].astype(F32)
    for r in range(1, 16):
        summed = summed + hr[r].astype(F32)
    summed = (summed * (1.0 / math.sqrt(32768))).astype(BF16)
    hs[...] = summed
    hall[me_m] = summed

    def ha_copy(r, owner):
        return remote(hs, hall.at[owner], ha_s.at[r], ha_r.at[r], mem=member(r))

    def tell(r, carry):
        ha_copy(r, me_m).start()
        return carry

    lax.fori_loop(1, 16, tell, 0)

    def ha_wait(r, carry):
        ha_copy(r, member(-r)).wait_recv()
        return carry

    lax.fori_loop(1, 16, ha_wait, 0)
    for j in range(16):
        lo = 24 * (j // 4)
        n = min(24, VARS - lo)
        head_out[lo : lo + n, 0, 128 * (j % 4) : 128 * (j % 4) + 128] = hall[j].astype(F32)[:n]

    turned.wait()
    for copy in row_copies + tile_copies[0] + tile_copies[1] + sib_copies:
        copy.wait_send()

    def far_done(j, carry):
        o = 3 - (j + 1) // 2
        even = lax.rem(j, 2)
        for h in range(2):
            for side in range(2):
                far_copy(h, side, j, o if side == 0 else -o, even if side == 0 else 1 - even)[
                    1
                ].wait_send()
        return carry

    lax.fori_loop(0, 5, far_done, 0)

    def members_done(r, carry):
        pred_copy(member(r))[1].wait_send()
        gs_copy(r).wait_send()
        hr_copy(r).wait_send()
        ha_copy(r, me_m).wait_send()
        return carry

    lax.fori_loop(1, 16, members_done, 0)


def back(score, w_head, out):
    out[...] = jnp.dot(score[...], w_head[...], preferred_element_type=F32).astype(BF16)


def shards(
    coarse_latents,
    send_rows,
    up_index,
    up_weight,
    neighbors,
    live_counts,
    area,
    fine_skip,
    targets,
    kernel_width,
    w_in,
    w_out,
    ln_gain,
    w_head,
):
    hbm = pl.BlockSpec(memory_space=pl.ANY)
    vmem = pl.BlockSpec(memory_space=pltpu.VMEM)
    smem = pl.BlockSpec(memory_space=pltpu.SMEM)
    dma = pltpu.SemaphoreType.DMA
    gscore, head = pl.pallas_call(
        kernel,
        name="decoder_tail",
        out_shape=(
            jax.ShapeDtypeStruct((2048, VARS), BF16),
            jax.ShapeDtypeStruct((VARS, 1, 512), F32),
        ),
        in_specs=[hbm, vmem, vmem, vmem, vmem, smem, vmem, hbm, vmem, vmem, hbm, hbm, vmem, vmem],
        out_specs=(hbm, vmem),
        scratch_shapes=[
            pltpu.VMEM((2, 3, 512, 256), BF16),
            pltpu.VMEM((2, 16, 128), jnp.int32),
            pltpu.VMEM((8, 2048, 512), BF16),
            pltpu.VMEM((2048, 512), BF16),
            pltpu.VMEM((6, 128, 128), F32),
            pltpu.VMEM((2, 8, 256, 256), BF16),
            pltpu.VMEM((2, 2, 5, 128, 256), BF16),
            pltpu.VMEM((2, 3, 128, 256), BF16),
            pltpu.VMEM((2048, 256), F32),
            pltpu.VMEM((2048, 512), F32),
            pltpu.VMEM((2048, 512), BF16),
            pltpu.VMEM((2, 2304, 256), BF16),
            pltpu.VMEM((2048, 512), BF16),
            pltpu.VMEM((1024, 512), BF16),
            pltpu.VMEM((512, 512), BF16),
            pltpu.VMEM((VP, 512), BF16),
            pltpu.VMEM((8, 128), F32),
            pltpu.VMEM((VP, 128), F32),
            pltpu.VMEM((VP, 128), F32),
            pltpu.VMEM((16, VP, 128), BF16),
            pltpu.VMEM((16, VP, 128), BF16),
            pltpu.VMEM((16, VP, 128), F32),
            pltpu.VMEM((16, VP, 128), BF16),
            pltpu.VMEM((VP, 2048), BF16),
            pltpu.VMEM((2048, VARS), BF16),
            pltpu.VMEM((16, 24, 128), BF16),
            pltpu.VMEM((16, 24, 128), BF16),
            pltpu.VMEM((24, 128), BF16),
            pltpu.VMEM((16, 24, 128), BF16),
            dma((6,)),
            dma((2, 2)),
            dma((2, 2)),
            dma((2,)),
            dma((2,)),
            dma((2, 2, 5)),
            dma((2, 3)),
            dma((2, 8, 2)),
            dma((2, 2)),
            dma((2, 2)),
            dma((16,)),
            dma((16,)),
            dma((16,)),
            dma((16,)),
            dma((16,)),
            dma((16,)),
            dma((16,)),
            dma((16,)),
        ],
        compiler_params=pltpu.CompilerParams(
            collective_id=0, has_side_effects=True, vmem_limit_bytes=60 * 1024 * 1024
        ),
    )(
        coarse_latents[0],
        send_rows[0],
        up_index,
        up_weight,
        neighbors,
        live_counts,
        area[None],
        fine_skip,
        targets,
        kernel_width[None],
        w_in,
        w_out,
        ln_gain[None],
        w_head.T,
    )
    grad_latent = pl.pallas_call(
        back,
        name="latent_gradient",
        out_shape=jax.ShapeDtypeStruct((2048, 512), BF16),
        grid=(4,),
        in_specs=[
            pl.BlockSpec((512, VARS), lambda i: (i, 0)),
            pl.BlockSpec((VARS, 512), lambda i: (0, 0)),
        ],
        out_specs=pl.BlockSpec((512, 512), lambda i: (i, 0)),
    )(gscore, w_head.T)
    return grad_latent[None], head.transpose(1, 2, 0)


def solution(mesh):
    in_specs = (
        P("mem", "dom", None),
        P("dom", None, None),
        P(None, "dom"),
        P(None, "dom"),
        P(None, "dom"),
        P("dom"),
        P("dom"),
        P("dom", None),
        P(None, "dom"),
        P(),
        P(),
        P(),
        P(),
        P(),
    )
    out_specs = (P("mem", "dom", None), P("dom", None, None))
    return jax.shard_map(
        shards, mesh=mesh, in_specs=in_specs, out_specs=out_specs, check_vma=False
    )
```

```python
import functools
import math

import jax
import jax.numpy as jnp
from jax import lax
from jax.experimental import pallas as pl
from jax.experimental.pallas import tpu as pltpu
from jax.sharding import PartitionSpec as P

F32 = jnp.float32
BF16 = jnp.bfloat16
VARS = 83
VP = 96
NT = (((1,), (1,)), ((), ()))


def lanes_of(row):
    return jnp.broadcast_to(row, (128, 128)).T


def kernel(
    coarse,
    send_rows,
    up_index_h,
    up_weight_h,
    neighbors_h,
    live,
    area_h,
    skip,
    targets_h,
    kwidth_h,
    w_in,
    w_out,
    gain_h,
    w_head_h,
    gs_out,
    head_out,
    own_rows,
    up_index,
    up_weight,
    neighbors,
    area,
    targets,
    kwidth,
    gain,
    w_head,
    tiles,
    rows,
    wbuf,
    nbuf,
    cols,
    recv,
    sbuf,
    sibbuf,
    acc,
    skipv,
    ext,
    hidden,
    win,
    wout,
    wht,
    kwp,
    inv_b,
    tgt,
    psend,
    pall,
    pf,
    ssend,
    gs,
    gst,
    hp,
    hr,
    hs,
    hall,
    loc_sem,
    tile_s,
    tile_r,
    rows_s,
    rows_r,
    g_s,
    sib_s,
    recv_sem,
    rim_s,
    rim_r,
    pred_s,
    pred_r,
    gs_s,
    gs_r,
    hr_s,
    hr_r,
    ha_s,
    ha_r,
):
    me_d = lax.axis_index("dom")
    me_m = lax.axis_index("mem")
    c = me_d // 2
    k = me_d - 2 * c
    other = 1 - k

    def chip(offset):
        return lax.rem(c + offset + 8, 8)

    def member(offset):
        return lax.rem(me_m + offset + 16, 16)

    def remote(src, dst, ssem, rsem, **device):
        return pltpu.make_async_remote_copy(
            src_ref=src,
            dst_ref=dst,
            send_sem=ssem,
            recv_sem=rsem,
            device_id=device,
            device_id_type=pl.DeviceIdType.MESH,
        )

    barrier = pltpu.get_barrier_semaphore()

    def greet(r, carry):
        pl.semaphore_signal(
            barrier,
            inc=1,
            device_id={"dom": lax.rem(me_d + r, 16)},
            device_id_type=pl.DeviceIdType.MESH,
        )
        pl.semaphore_signal(
            barrier, inc=1, device_id={"mem": member(r)}, device_id_type=pl.DeviceIdType.MESH
        )
        return carry

    lax.fori_loop(1, 16, greet, 0)
    my_share = pl.ds(pl.multiple_of(me_m * 128, 128), 128)
    loads = [
        pltpu.make_async_copy(src, dst, loc_sem.at[i])
        for i, (src, dst) in enumerate(
            (
                (send_rows, own_rows),
                (coarse.at[:, :256], tiles.at[0, 0]),
                (coarse.at[:, 256:], tiles.at[1, 0]),
                (neighbors_h, neighbors),
                (w_head_h, w_head),
                (kwidth_h, kwidth),
                (targets_h.at[:, my_share], targets),
                (area_h.at[:, my_share], area),
                (up_index_h, up_index),
                (up_weight_h, up_weight),
                (gain_h, gain),
                (skip, skipv),
                (w_in, win),
                (w_out, wout),
            )
        )
    ]
    for load in loads:
        load.start()
    pl.semaphore_wait(barrier, 30)

    next_to = (chip(1) * 2 + k, chip(-1) * 2 + k)

    def pass_on(h, src, slot, side):
        return remote(
            src,
            tiles.at[h, slot],
            tile_s.at[h, slot - 1],
            tile_r.at[h, slot - 1],
            dom=next_to[side],
        )

    def pass_rows(src, slot, side):
        return remote(
            src,
            rows.at[slot - 1],
            rows_s.at[slot - 1],
            rows_r.at[slot - 1],
            dom=next_to[side],
        )

    row_copies = [pass_rows(send_rows, 1 + side, side) for side in range(2)]
    near = [
        [
            pass_on(h, coarse.at[:, 256 * h : 256 * h + 256], 1 + side, side)
            for side in range(2)
        ]
        for h in range(2)
    ]
    for copy in row_copies + near[0] + near[1]:
        copy.start()

    lane = lax.broadcasted_iota(jnp.int32, (128, 128), 1).astype(F32)

    def picked(table, tile, dest):
        row = table[pl.ds(dest, 1), :].astype(F32)
        col = lanes_of(row)
        hot = jnp.concatenate(
            [jnp.where(col == lane + 128.0 * q, 1.0, 0.0).astype(BF16) for q in range(4)], axis=1
        )
        return jnp.dot(hot, tile[...], preferred_element_type=F32).astype(BF16)

    my_rows = pl.ds(pl.multiple_of(k * 128, 128), 128)

    def at_home(table, slot, rel):
        for h in range(2):
            tile = tiles.at[h, slot]
            lanes = slice(256 * h, 256 * h + 256)
            sibbuf[h, slot] = picked(table, tile, me_d + other - k)
            copy = remote(
                sibbuf.at[h, slot],
                recv.at[rel, my_rows, lanes],
                sib_s.at[h, slot],
                recv_sem.at[h, rel, k],
                dom=c * 2 + other,
            )
            copy.start()
            recv[rel, my_rows, lanes] = picked(table, tile, me_d)
            sib_copies.append(copy)

    sib_copies = []
    for load in loads[:3]:
        load.wait()
    at_home(own_rows, 0, 0)

    def weights_of(t, carry):
        at = pl.ds(pl.multiple_of(t * 128, 128), 128)
        for j in range(3):
            cols[j] = lanes_of(up_index[j : j + 1, at].astype(F32))
            cols[3 + j] = lanes_of(up_weight[j : j + 1, at])

        def part(s, carry):
            sub = pl.ds(pl.multiple_of(s * 32, 32), 32)
            out = pl.ds(pl.multiple_of(t * 128 + s * 32, 32), 32)
            idx = [cols[j, sub, :] for j in range(3)]
            wgt = [cols[3 + j, sub, :] for j in range(3)]
            base = lax.broadcasted_iota(jnp.int32, (32, 128), 1).astype(F32)
            for q in range(16):
                slot = base + 128.0 * q
                w = (
                    jnp.where(idx[0] == slot, wgt[0], 0.0)
                    + jnp.where(idx[1] == slot, wgt[1], 0.0)
                    + jnp.where(idx[2] == slot, wgt[2], 0.0)
                )
                hi = w.astype(BF16)
                lo = (w - hi.astype(F32)).astype(BF16)
                wbuf[q // 2, out, (q % 2) * 128 : (q % 2) * 128 + 128] = hi
                wbuf[q // 2, out, 256 + (q % 2) * 128 : 384 + (q % 2) * 128] = lo
            return carry

        lax.fori_loop(0, 4, part, 0)
        return carry

    def counts_of(t, carry):
        at = pl.ds(pl.multiple_of(t * 128, 128), 128)
        shift = ((t // 2) * 256).astype(F32)
        for j in range(6):
            cols[j] = lanes_of(neighbors[j : j + 1, at].astype(F32) - shift)

        def part(s, carry):
            sub = pl.ds(pl.multiple_of(s * 32, 32), 32)
            out = pl.ds(pl.multiple_of(t * 128 + s * 32, 32), 32)
            idx = [cols[j, sub, :] for j in range(6)]
            base = lax.broadcasted_iota(jnp.int32, (32, 128), 1).astype(F32)
            for q in range(4):
                spot = base + 128.0 * q
                total = jnp.where(idx[0] == spot, 1.0, 0.0)
                for j in range(1, 6):
                    total = total + jnp.where(idx[j] == spot, 1.0, 0.0)
                nbuf[out, q * 128 : q * 128 + 128] = total.astype(BF16)
            return carry

        lax.fori_loop(0, 4, part, 0)
        return carry

    for load in loads[3:8]:
        load.wait()
    wht[...] = jnp.zeros((VP, 512), BF16)
    wht[:VARS, :] = w_head[...]
    kwp[...] = jnp.ones((8, 128), F32)
    kwp[0:1, :VARS] = kwidth[...]
    width = kwp[0:1, :]
    inv_b[...] = lanes_of(1.0 / (width * width))[:VP]
    tgt[...] = jnp.zeros((VP, 128), F32)
    tgt[:VARS, :] = targets[...].astype(F32)

    lax.fori_loop(0, 16, counts_of, 0)

    for copy in row_copies:
        copy.wait_recv()
    row_copies += [pass_rows(rows.at[side], 3 + side, side) for side in range(2)]
    for copy in row_copies[2:]:
        copy.start()
    next_one = []

    def forward(h):
        for side in range(2):
            near[h][side].wait_recv()
            copy = pass_on(h, tiles.at[h, 1 + side], 3 + side, side)
            copy.start()
            next_one.append(copy)

    forward(0)
    for load in loads[8:10]:
        load.wait()
    lax.fori_loop(0, 8, weights_of, 0)
    forward(1)
    at_home(rows.at[0], 1, 7)
    at_home(rows.at[1], 2, 1)
    lax.fori_loop(8, 16, weights_of, 0)
    for load in loads[10:]:
        load.wait()

    def far_copy(h, side, j, o, kd):
        dest = chip(o) * 2 + kd
        rel = 4 + (j + 1) // 2 if side == 0 else 4 - (j + 1) // 2
        return dest, remote(
            sbuf.at[h, side, j],
            recv.at[rel, my_rows, 256 * h : 256 * h + 256],
            g_s.at[h, side, j],
            recv_sem.at[h, rel, k],
            dom=dest,
        )

    def send_far(h):
        for copy in next_one[2 * h : 2 * h + 2]:
            copy.wait_recv()

        def both_ways(j, carry):
            o = 2 - (j + 1) // 2
            even = lax.rem(j, 2)
            for side in range(2):
                dest, copy = far_copy(
                    h, side, j, o if side == 0 else -o, even if side == 0 else 1 - even
                )
                sbuf[h, side, j] = picked(rows.at[2 + side], tiles.at[h, 3 + side], dest)
                copy.start()
            return carry

        lax.fori_loop(0, 3, both_ways, 0)

    def arrived(rel, kb):
        half = pl.ds(pl.multiple_of(kb * 128, 128), 128)
        for h in range(2):
            remote(
                sibbuf.at[h, 0],
                recv.at[rel, half, 256 * h : 256 * h + 256],
                sib_s.at[h, 0],
                recv_sem.at[h, rel, kb],
                dom=c * 2 + other,
            ).wait_recv()

    def added(rels, t):
        at = pl.ds(pl.multiple_of(t * 512, 512), 512)
        total = skipv[at, :].astype(F32) if rels[0] == 0 else acc[at, :]
        for rel in rels:
            here = chip(rel)
            table = recv[rel]
            total = total + jnp.dot(wbuf[here, at, :256], table, preferred_element_type=F32)
            total = total + jnp.dot(wbuf[here, at, 256:], table, preferred_element_type=F32)
        return at, total

    def unpool(rels):
        for rel in rels:
            arrived(rel, other)
            if rel in (3, 4, 5):
                arrived(rel, k)

        def accumulate(t, carry, rels=rels):
            at, total = added(rels, t)
            acc[at, :] = total
            return carry

        lax.fori_loop(0, 4, accumulate, 0)

    for copy in row_copies[2:]:
        copy.wait_recv()
    send_far(0)
    unpool((0,))
    unpool((7, 1))
    send_far(1)
    at_home(rows.at[2], 3, 6)
    at_home(rows.at[3], 4, 2)
    unpool((6, 2))
    unpool((4,))
    for rel in (5, 3):
        arrived(rel, 0)
        arrived(rel, 1)

    def finish(t, carry):
        total = added((5, 3), t)[1]
        ext[pl.ds(pl.multiple_of(t * 512 + 128, 128), 512), :] = total.astype(BF16)
        return carry

    lax.fori_loop(0, 2, lambda t, carry: finish(t * 3, carry), 0)
    rims = [
        remote(
            ext.at[pl.ds(2048, 128)],
            ext.at[pl.ds(0, 128)],
            rim_s.at[0],
            rim_r.at[0],
            dom=lax.rem(me_d + 1, 16),
        ),
        remote(
            ext.at[pl.ds(128, 128)],
            ext.at[pl.ds(2176, 128)],
            rim_s.at[1],
            rim_r.at[1],
            dom=lax.rem(me_d + 15, 16),
        ),
    ]
    for rim in rims:
        rim.start()
    lax.fori_loop(1, 3, finish, 0)

    gain_row = gain[...]

    def pred_copy(j):
        r = lax.rem(j - me_m + 16, 16)
        return r, remote(psend.at[j], pall.at[r], pred_s.at[r], pred_r.at[r], mem=j)

    def dense(i, carry):
        x = ext[pl.ds(pl.multiple_of(i * 512 + 128, 128), 512), :]
        parts = []
        for s in range(2):
            start = pl.multiple_of(i * 512 + s * 256, 256)
            total = jnp.dot(
                nbuf[pl.ds(start, 256), :], ext[pl.ds(start, 512), :], preferred_element_type=F32
            )
            parts.append((total * (1.0 / 6)).astype(BF16))
        agg = jnp.concatenate(parts, axis=0)
        pre = jnp.dot(x, win[:512], preferred_element_type=F32) + jnp.dot(
            agg, win[512:], preferred_element_type=F32
        )
        half = 0.5 * pre
        act = (half + half * jnp.tanh(half)).astype(BF16)
        upd = jnp.dot(act, wout[...], preferred_element_type=F32)
        mean = jnp.sum(upd, axis=1, keepdims=True) * (1.0 / 512)
        centred = upd - mean
        var = jnp.sum(centred * centred, axis=1, keepdims=True) * (1.0 / 512)
        h = (x.astype(F32) + centred * lax.rsqrt(var + 1e-05) * gain_row).astype(BF16)
        hidden[pl.ds(pl.multiple_of(i * 512, 512), 512), :] = h
        pred = lax.dot_general(wht[...], h, NT, preferred_element_type=F32).astype(BF16)
        for s in range(4):
            j = 4 * i + s
            r, copy = pred_copy(j)
            psend[j] = pred[:, s * 128 : s * 128 + 128]

            @pl.when(r != 0)
            def _():
                copy.start()

            @pl.when(r == 0)
            def _():
                pall[0] = psend[j]

        return carry

    lax.fori_loop(1, 3, dense, 0)
    for rim in rims:
        rim.wait()

    @pl.when(me_d == 0)
    def _():
        ext[pl.ds(0, 128), :] = jnp.zeros((128, 512), BF16)

    @pl.when(me_d == 15)
    def _():
        ext[pl.ds(2176, 128), :] = jnp.zeros((128, 512), BF16)

    lax.fori_loop(0, 2, lambda t, carry: dense(t * 3, carry), 0)

    def pred_wait(r, carry):
        remote(psend.at[0], pall.at[r], pred_s.at[r], pred_r.at[r], mem=member(r)).wait_recv()
        return carry

    lax.fori_loop(1, 16, pred_wait, 0)

    def widen(r, carry):
        pf[r] = pall[r].astype(F32)
        return carry

    lax.fori_loop(0, 16, widen, 0)
    place = lax.broadcasted_iota(jnp.int32, (1, 128), 1) + me_m * 128
    weight = jnp.broadcast_to(jnp.where(place < live[0], area[...], 0.0), (8, 128))

    def scores(q, carry):
        at = pl.ds(pl.multiple_of(q * 8, 8), 8)
        inv = inv_b[at, :]
        halved = -0.5 * inv
        p = [pf[i, at, :] for i in range(16)]
        t = tgt[at, :]
        total = [None] * 16
        for i in range(16):
            for j in range(i):
                e = p[i] - p[j]
                s = e * jnp.exp(e * e * halved)
                total[i] = s if total[i] is None else total[i] + s
                total[j] = -s if total[j] is None else total[j] - s
        scale = weight * inv
        for i in range(16):
            e = p[i] - t
            pf[i, at, :] = scale * (e * jnp.exp(e * e * halved) - total[i] * (1.0 / 16))
        return carry


    def gs_copy(v, r, share, back):
        return remote(
            ssend.at[r, pl.ds(48 * v, 48)],
            gs.at[pl.ds(48 * v, 48), share],
            gs_s.at[v, r],
            gs_r.at[v, r],
            mem=back,
        )

    for v in range(2):
        lax.fori_loop(6 * v, 6 * v + 6, scores, 0)

        def give_back(r, carry, v=v):
            ssend[r, 48 * v : 48 * v + 48, :] = pf[r, 48 * v : 48 * v + 48, :].astype(BF16)
            gs_copy(v, r, my_share, member(-r)).start()
            return carry

        lax.fori_loop(1, 16, give_back, 0)
        gs[48 * v : 48 * v + 48, my_share] = pf[0, 48 * v : 48 * v + 48, :].astype(BF16)

    def gs_wait(r, carry):
        share = pl.ds(pl.multiple_of(member(r) * 128, 128), 128)
        for v in range(2):
            gs_copy(v, r, share, member(r)).wait_recv()
        return carry

    lax.fori_loop(1, 16, gs_wait, 0)

    head = jnp.dot(gs[...], hidden[...], preferred_element_type=F32)
    for j in range(16):
        lo, left = 24 * (j // 4), 128 * (j % 4)
        hp[j] = head[lo : lo + 24, left : left + 128].astype(BF16)

    def hr_copy(r):
        return remote(hp.at[member(r)], hr.at[r], hr_s.at[r], hr_r.at[r], mem=member(r))

    def spread(r, carry):
        hr_copy(r).start()
        return carry

    lax.fori_loop(1, 16, spread, 0)
    hr[0] = hp[me_m]

    def turn(j, carry):
        at = pl.ds(pl.multiple_of(j * 128, 128), 128)
        gst[at, :] = gs[:, at].astype(F32).T[:, :VARS].astype(BF16)
        return carry

    lax.fori_loop(0, 16, turn, 0)
    turned = pltpu.make_async_copy(gst, gs_out, loc_sem.at[14])
    turned.start()

    def hr_wait(r, carry):
        hr_copy(r).wait_recv()
        return carry

    lax.fori_loop(1, 16, hr_wait, 0)
    summed = hr[0].astype(F32)
    for r in range(1, 16):
        summed = summed + hr[r].astype(F32)
    summed = (summed * (1.0 / math.sqrt(32768))).astype(BF16)
    hs[...] = summed
    hall[me_m] = summed

    def ha_copy(r, owner):
        return remote(hs, hall.at[owner], ha_s.at[r], ha_r.at[r], mem=member(r))

    def tell(r, carry):
        ha_copy(r, me_m).start()
        return carry

    lax.fori_loop(1, 16, tell, 0)

    def ha_wait(r, carry):
        ha_copy(r, member(-r)).wait_recv()
        return carry

    lax.fori_loop(1, 16, ha_wait, 0)
    for j in range(16):
        lo = 24 * (j // 4)
        n = min(24, VARS - lo)
        head_out[lo : lo + n, 0, 128 * (j % 4) : 128 * (j % 4) + 128] = hall[j].astype(F32)[:n]

    turned.wait()
    for copy in row_copies + near[0] + near[1] + next_one + sib_copies:
        copy.wait_send()

    def far_done(j, carry):
        o = 2 - (j + 1) // 2
        even = lax.rem(j, 2)
        for h in range(2):
            for side in range(2):
                far_copy(h, side, j, o if side == 0 else -o, even if side == 0 else 1 - even)[
                    1
                ].wait_send()
        return carry

    lax.fori_loop(0, 3, far_done, 0)

    def members_done(r, carry):
        pred_copy(member(r))[1].wait_send()
        for v in range(2):
            gs_copy(v, r, my_share, member(-r)).wait_send()
        hr_copy(r).wait_send()
        ha_copy(r, me_m).wait_send()
        return carry

    lax.fori_loop(1, 16, members_done, 0)


def shards(
    coarse_latents,
    send_rows,
    up_index,
    up_weight,
    neighbors,
    live_counts,
    area,
    fine_skip,
    targets,
    kernel_width,
    w_in,
    w_out,
    ln_gain,
    w_head,
):
    hbm = pl.BlockSpec(memory_space=pl.ANY)
    vmem = pl.BlockSpec(memory_space=pltpu.VMEM)
    smem = pl.BlockSpec(memory_space=pltpu.SMEM)
    dma = pltpu.SemaphoreType.DMA
    gscore, head = pl.pallas_call(
        kernel,
        name="decoder_tail",
        out_shape=(
            jax.ShapeDtypeStruct((2048, VARS), BF16),
            jax.ShapeDtypeStruct((VARS, 1, 512), F32),
        ),
        in_specs=[hbm] * 5 + [smem] + [hbm] * 8,
        out_specs=(hbm, vmem),
        scratch_shapes=[
            pltpu.VMEM((16, 128), jnp.int32),
            pltpu.VMEM((3, 2048), jnp.int32),
            pltpu.VMEM((3, 2048), F32),
            pltpu.VMEM((6, 2048), jnp.int32),
            pltpu.VMEM((1, 128), F32),
            pltpu.VMEM((VARS, 128), BF16),
            pltpu.VMEM((1, VARS), F32),
            pltpu.VMEM((1, 512), F32),
            pltpu.VMEM((VARS, 512), BF16),
            pltpu.VMEM((2, 5, 512, 256), BF16),
            pltpu.VMEM((4, 16, 128), jnp.int32),
            pltpu.VMEM((8, 2048, 512), BF16),
            pltpu.VMEM((2048, 512), BF16),
            pltpu.VMEM((6, 128, 128), F32),
            pltpu.VMEM((8, 256, 512), BF16),
            pltpu.VMEM((2, 2, 3, 128, 256), BF16),
            pltpu.VMEM((2, 5, 128, 256), BF16),
            pltpu.VMEM((2048, 512), F32),
            pltpu.VMEM((2048, 512), BF16),
            pltpu.VMEM((2304, 512), BF16),
            pltpu.VMEM((2048, 512), BF16),
            pltpu.VMEM((1024, 512), BF16),
            pltpu.VMEM((512, 512), BF16),
            pltpu.VMEM((VP, 512), BF16),
            pltpu.VMEM((8, 128), F32),
            pltpu.VMEM((VP, 128), F32),
            pltpu.VMEM((VP, 128), F32),
            pltpu.VMEM((16, VP, 128), BF16),
            pltpu.VMEM((16, VP, 128), BF16),
            pltpu.VMEM((16, VP, 128), F32),
            pltpu.VMEM((16, VP, 128), BF16),
            pltpu.VMEM((VP, 2048), BF16),
            pltpu.VMEM((2048, VARS), BF16),
            pltpu.VMEM((16, 24, 128), BF16),
            pltpu.VMEM((16, 24, 128), BF16),
            pltpu.VMEM((24, 128), BF16),
            pltpu.VMEM((16, 24, 128), BF16),
            dma((15,)),
            dma((2, 4)),
            dma((2, 4)),
            dma((4,)),
            dma((4,)),
            dma((2, 2, 3)),
            dma((2, 5)),
            dma((2, 8, 2)),
            dma((2,)),
            dma((2,)),
            dma((16,)),
            dma((16,)),
            dma((2, 16)),
            dma((2, 16)),
            dma((16,)),
            dma((16,)),
            dma((16,)),
            dma((16,)),
        ],
        compiler_params=pltpu.CompilerParams(
            collective_id=0, has_side_effects=True, vmem_limit_bytes=60 * 1024 * 1024
        ),
    )(
        coarse_latents[0],
        send_rows[0],
        up_index,
        up_weight,
        neighbors,
        live_counts,
        area[None],
        fine_skip,
        targets,
        kernel_width[None],
        w_in,
        w_out,
        ln_gain[None],
        w_head.T,
    )
    grad_latent = lax.dot_general(
        gscore, w_head, (((1,), (1,)), ((), ())), preferred_element_type=F32
    ).astype(BF16)
    return grad_latent[None], head.transpose(1, 2, 0)


def solution(mesh):
    in_specs = (
        P("mem", "dom", None),
        P("dom", None, None),
        P(None, "dom"),
        P(None, "dom"),
        P(None, "dom"),
        P("dom"),
        P("dom"),
        P("dom", None),
        P(None, "dom"),
        P(),
        P(),
        P(),
        P(),
        P(),
    )
    out_specs = (P("mem", "dom", None), P("dom", None, None))
    return jax.shard_map(
        shards, mesh=mesh, in_specs=in_specs, out_specs=out_specs, check_vma=False
    )
```

```python
import functools
import math

import jax
import jax.numpy as jnp
from jax import lax
from jax.experimental import pallas as pl
from jax.experimental.pallas import tpu as pltpu
from jax.sharding import PartitionSpec as P

F32 = jnp.float32
BF16 = jnp.bfloat16
VARS = 83
VP = 96
NT = (((1,), (1,)), ((), ()))


def lanes_of(row):
    return jnp.broadcast_to(row, (128, 128)).T


def kernel(
    coarse,
    send_rows,
    up_index_h,
    up_weight_h,
    neighbors_h,
    live,
    area_h,
    skip,
    targets_h,
    kwidth_h,
    w_in,
    w_out,
    gain_h,
    w_head_h,
    grad_out,
    head_out,
    own_rows,
    up_index,
    up_weight,
    neighbors,
    area,
    targets,
    kwidth,
    gain,
    w_head,
    tiles,
    rows,
    wbuf,
    nbuf,
    cols,
    recv,
    sbuf,
    sibbuf,
    acc,
    skipv,
    ext,
    hidden,
    win,
    wout,
    wht,
    kwp,
    inv_b,
    tgt,
    psend,
    pall,
    pf,
    ssend,
    gs,
    hp,
    hr,
    hs,
    hall,
    loc_sem,
    grad_sem,
    tile_s,
    tile_r,
    rows_s,
    rows_r,
    g_s,
    sib_s,
    recv_sem,
    rim_s,
    rim_r,
    pred_s,
    pred_r,
    gs_s,
    gs_r,
    hr_s,
    hr_r,
    ha_s,
    ha_r,
):
    me_d = lax.axis_index("dom")
    me_m = lax.axis_index("mem")
    c = me_d // 2
    k = me_d - 2 * c
    other = 1 - k

    def chip(offset):
        return lax.rem(c + offset + 8, 8)

    def member(offset):
        return lax.rem(me_m + offset + 16, 16)

    def remote(src, dst, ssem, rsem, **device):
        return pltpu.make_async_remote_copy(
            src_ref=src,
            dst_ref=dst,
            send_sem=ssem,
            recv_sem=rsem,
            device_id=device,
            device_id_type=pl.DeviceIdType.MESH,
        )

    barrier = pltpu.get_barrier_semaphore()

    def greet(r, carry):
        pl.semaphore_signal(
            barrier,
            inc=1,
            device_id={"dom": lax.rem(me_d + r, 16)},
            device_id_type=pl.DeviceIdType.MESH,
        )
        pl.semaphore_signal(
            barrier, inc=1, device_id={"mem": member(r)}, device_id_type=pl.DeviceIdType.MESH
        )
        return carry

    lax.fori_loop(1, 16, greet, 0)
    my_share = pl.ds(pl.multiple_of(me_m * 128, 128), 128)
    loads = [
        pltpu.make_async_copy(src, dst, loc_sem.at[i])
        for i, (src, dst) in enumerate(
            (
                (send_rows, own_rows),
                (coarse.at[:, :256], tiles.at[0, 0]),
                (coarse.at[:, 256:], tiles.at[1, 0]),
                (neighbors_h, neighbors),
                (w_head_h, w_head),
                (kwidth_h, kwidth),
                (targets_h.at[:, my_share], targets),
                (area_h.at[:, my_share], area),
                (up_index_h, up_index),
                (up_weight_h, up_weight),
                (gain_h, gain),
                (skip, skipv),
                (w_in, win),
                (w_out, wout),
            )
        )
    ]
    for load in loads:
        load.start()
    pl.semaphore_wait(barrier, 30)

    next_to = (chip(1) * 2 + k, chip(-1) * 2 + k)

    def pass_on(h, src, slot, side):
        return remote(
            src,
            tiles.at[h, slot],
            tile_s.at[h, slot - 1],
            tile_r.at[h, slot - 1],
            dom=next_to[side],
        )

    def pass_rows(src, slot, side):
        return remote(
            src,
            rows.at[slot - 1],
            rows_s.at[slot - 1],
            rows_r.at[slot - 1],
            dom=next_to[side],
        )

    row_copies = [pass_rows(send_rows, 1 + side, side) for side in range(2)]
    near = [
        [
            pass_on(h, coarse.at[:, 256 * h : 256 * h + 256], 1 + side, side)
            for side in range(2)
        ]
        for h in range(2)
    ]
    for copy in row_copies + near[0] + near[1]:
        copy.start()

    lane = lax.broadcasted_iota(jnp.int32, (128, 128), 1).astype(F32)

    def picked(table, tile, dest):
        row = table[pl.ds(dest, 1), :].astype(F32)
        col = lanes_of(row)
        hot = jnp.concatenate(
            [jnp.where(col == lane + 128.0 * q, 1.0, 0.0).astype(BF16) for q in range(4)], axis=1
        )
        return jnp.dot(hot, tile[...], preferred_element_type=F32).astype(BF16)

    my_rows = pl.ds(pl.multiple_of(k * 128, 128), 128)

    def at_home(table, slot, rel):
        for h in range(2):
            tile = tiles.at[h, slot]
            lanes = slice(256 * h, 256 * h + 256)
            sibbuf[h, slot] = picked(table, tile, me_d + other - k)
            copy = remote(
                sibbuf.at[h, slot],
                recv.at[rel, my_rows, lanes],
                sib_s.at[h, slot],
                recv_sem.at[h, rel, k],
                dom=c * 2 + other,
            )
            copy.start()
            recv[rel, my_rows, lanes] = picked(table, tile, me_d)
            sib_copies.append(copy)

    sib_copies = []
    for load in loads[:3]:
        load.wait()
    at_home(own_rows, 0, 0)

    def weights_of(t, carry):
        at = pl.ds(pl.multiple_of(t * 128, 128), 128)
        for j in range(3):
            cols[j] = lanes_of(up_index[j : j + 1, at].astype(F32))
            cols[3 + j] = lanes_of(up_weight[j : j + 1, at])

        def part(s, carry):
            sub = pl.ds(pl.multiple_of(s * 32, 32), 32)
            out = pl.ds(pl.multiple_of(t * 128 + s * 32, 32), 32)
            idx = [cols[j, sub, :] for j in range(3)]
            wgt = [cols[3 + j, sub, :] for j in range(3)]
            base = lax.broadcasted_iota(jnp.int32, (32, 128), 1).astype(F32)
            for q in range(16):
                slot = base + 128.0 * q
                w = (
                    jnp.where(idx[0] == slot, wgt[0], 0.0)
                    + jnp.where(idx[1] == slot, wgt[1], 0.0)
                    + jnp.where(idx[2] == slot, wgt[2], 0.0)
                )
                hi = w.astype(BF16)
                lo = (w - hi.astype(F32)).astype(BF16)
                wbuf[q // 2, out, (q % 2) * 128 : (q % 2) * 128 + 128] = hi
                wbuf[q // 2, out, 256 + (q % 2) * 128 : 384 + (q % 2) * 128] = lo
            return carry

        lax.fori_loop(0, 4, part, 0)
        return carry

    def counts_of(t, carry):
        at = pl.ds(pl.multiple_of(t * 128, 128), 128)
        shift = ((t // 2) * 256).astype(F32)
        for j in range(6):
            cols[j] = lanes_of(neighbors[j : j + 1, at].astype(F32) - shift)

        def part(s, carry):
            sub = pl.ds(pl.multiple_of(s * 32, 32), 32)
            out = pl.ds(pl.multiple_of(t * 128 + s * 32, 32), 32)
            idx = [cols[j, sub, :] for j in range(6)]
            base = lax.broadcasted_iota(jnp.int32, (32, 128), 1).astype(F32)
            for q in range(4):
                spot = base + 128.0 * q
                total = jnp.where(idx[0] == spot, 1.0, 0.0)
                for j in range(1, 6):
                    total = total + jnp.where(idx[j] == spot, 1.0, 0.0)
                nbuf[out, q * 128 : q * 128 + 128] = total.astype(BF16)
            return carry

        lax.fori_loop(0, 4, part, 0)
        return carry

    for load in loads[3:8]:
        load.wait()
    wht[...] = jnp.zeros((VP, 512), BF16)
    wht[:VARS, :] = w_head[...]
    kwp[...] = jnp.ones((8, 128), F32)
    kwp[0:1, :VARS] = kwidth[...]
    width = kwp[0:1, :]
    inv_b[...] = lanes_of(1.0 / (width * width))[:VP]
    tgt[...] = jnp.zeros((VP, 128), F32)
    tgt[:VARS, :] = targets[...].astype(F32)

    lax.fori_loop(0, 16, counts_of, 0)

    for copy in row_copies:
        copy.wait_recv()
    row_copies += [pass_rows(rows.at[side], 3 + side, side) for side in range(2)]
    for copy in row_copies[2:]:
        copy.start()
    next_one = []

    def forward(h):
        for side in range(2):
            near[h][side].wait_recv()
            copy = pass_on(h, tiles.at[h, 1 + side], 3 + side, side)
            copy.start()
            next_one.append(copy)

    forward(0)
    for load in loads[8:10]:
        load.wait()
    lax.fori_loop(0, 8, weights_of, 0)
    forward(1)
    at_home(rows.at[0], 1, 7)
    at_home(rows.at[1], 2, 1)
    lax.fori_loop(8, 16, weights_of, 0)
    for load in loads[10:]:
        load.wait()

    def far_copy(h, side, j, o, kd):
        dest = chip(o) * 2 + kd
        rel = 4 + (j + 1) // 2 if side == 0 else 4 - (j + 1) // 2
        return dest, remote(
            sbuf.at[h, side, j],
            recv.at[rel, my_rows, 256 * h : 256 * h + 256],
            g_s.at[h, side, j],
            recv_sem.at[h, rel, k],
            dom=dest,
        )

    def send_far(h):
        for copy in next_one[2 * h : 2 * h + 2]:
            copy.wait_recv()

        def both_ways(j, carry):
            o = 2 - (j + 1) // 2
            even = lax.rem(j, 2)
            for side in range(2):
                dest, copy = far_copy(
                    h, side, j, o if side == 0 else -o, even if side == 0 else 1 - even
                )
                sbuf[h, side, j] = picked(rows.at[2 + side], tiles.at[h, 3 + side], dest)
                copy.start()
            return carry

        lax.fori_loop(0, 3, both_ways, 0)

    def arrived(rel, kb):
        half = pl.ds(pl.multiple_of(kb * 128, 128), 128)
        for h in range(2):
            remote(
                sibbuf.at[h, 0],
                recv.at[rel, half, 256 * h : 256 * h + 256],
                sib_s.at[h, 0],
                recv_sem.at[h, rel, kb],
                dom=c * 2 + other,
            ).wait_recv()

    def added(rels, t):
        at = pl.ds(pl.multiple_of(t * 512, 512), 512)
        total = skipv[at, :].astype(F32) if rels[0] == 0 else acc[at, :]
        for rel in rels:
            here = chip(rel)
            table = recv[rel]
            total = total + jnp.dot(wbuf[here, at, :256], table, preferred_element_type=F32)
            total = total + jnp.dot(wbuf[here, at, 256:], table, preferred_element_type=F32)
        return at, total

    def unpool(rels):
        for rel in rels:
            arrived(rel, other)
            if rel in (3, 4, 5):
                arrived(rel, k)

        def accumulate(t, carry, rels=rels):
            at, total = added(rels, t)
            acc[at, :] = total
            return carry

        lax.fori_loop(0, 4, accumulate, 0)

    for copy in row_copies[2:]:
        copy.wait_recv()
    send_far(0)
    unpool((0,))
    unpool((7, 1))
    send_far(1)
    at_home(rows.at[2], 3, 6)
    at_home(rows.at[3], 4, 2)
    unpool((6, 2))
    unpool((4,))
    for rel in (5, 3):
        arrived(rel, 0)
        arrived(rel, 1)

    def finish(t, carry):
        total = added((5, 3), t)[1]
        ext[pl.ds(pl.multiple_of(t * 512 + 128, 128), 512), :] = total.astype(BF16)
        return carry

    lax.fori_loop(0, 2, lambda t, carry: finish(t * 3, carry), 0)
    rims = [
        remote(
            ext.at[pl.ds(2048, 128)],
            ext.at[pl.ds(0, 128)],
            rim_s.at[0],
            rim_r.at[0],
            dom=lax.rem(me_d + 1, 16),
        ),
        remote(
            ext.at[pl.ds(128, 128)],
            ext.at[pl.ds(2176, 128)],
            rim_s.at[1],
            rim_r.at[1],
            dom=lax.rem(me_d + 15, 16),
        ),
    ]
    for rim in rims:
        rim.start()
    lax.fori_loop(1, 3, finish, 0)

    gain_row = gain[...]

    def pred_copy(j):
        r = lax.rem(j - me_m + 16, 16)
        return r, remote(psend.at[j], pall.at[r], pred_s.at[r], pred_r.at[r], mem=j)

    def dense(i, carry):
        x = ext[pl.ds(pl.multiple_of(i * 512 + 128, 128), 512), :]
        parts = []
        for s in range(2):
            start = pl.multiple_of(i * 512 + s * 256, 256)
            total = jnp.dot(
                nbuf[pl.ds(start, 256), :], ext[pl.ds(start, 512), :], preferred_element_type=F32
            )
            parts.append((total * (1.0 / 6)).astype(BF16))
        agg = jnp.concatenate(parts, axis=0)
        pre = jnp.dot(x, win[:512], preferred_element_type=F32) + jnp.dot(
            agg, win[512:], preferred_element_type=F32
        )
        half = 0.5 * pre
        act = (half + half * jnp.tanh(half)).astype(BF16)
        upd = jnp.dot(act, wout[...], preferred_element_type=F32)
        mean = jnp.sum(upd, axis=1, keepdims=True) * (1.0 / 512)
        centred = upd - mean
        var = jnp.sum(centred * centred, axis=1, keepdims=True) * (1.0 / 512)
        h = (x.astype(F32) + centred * lax.rsqrt(var + 1e-05) * gain_row).astype(BF16)
        hidden[pl.ds(pl.multiple_of(i * 512, 512), 512), :] = h
        pred = lax.dot_general(wht[...], h, NT, preferred_element_type=F32).astype(BF16)
        for s in range(4):
            j = 4 * i + s
            r, copy = pred_copy(j)
            psend[j] = pred[:, s * 128 : s * 128 + 128]

            @pl.when(r != 0)
            def _():
                copy.start()

            @pl.when(r == 0)
            def _():
                pall[0] = psend[j]

        return carry

    lax.fori_loop(1, 3, dense, 0)
    for rim in rims:
        rim.wait()

    @pl.when(me_d == 0)
    def _():
        ext[pl.ds(0, 128), :] = jnp.zeros((128, 512), BF16)

    @pl.when(me_d == 15)
    def _():
        ext[pl.ds(2176, 128), :] = jnp.zeros((128, 512), BF16)

    lax.fori_loop(0, 2, lambda t, carry: dense(t * 3, carry), 0)

    def pred_wait(r, carry):
        remote(psend.at[0], pall.at[r], pred_s.at[r], pred_r.at[r], mem=member(r)).wait_recv()
        return carry

    lax.fori_loop(1, 16, pred_wait, 0)

    def widen(r, carry):
        pf[r] = pall[r].astype(F32)
        return carry

    lax.fori_loop(0, 16, widen, 0)
    place = lax.broadcasted_iota(jnp.int32, (1, 128), 1) + me_m * 128
    weight = jnp.broadcast_to(jnp.where(place < live[0], area[...], 0.0), (8, 128))

    def scores(q, carry):
        at = pl.ds(pl.multiple_of(q * 8, 8), 8)
        inv = inv_b[at, :]
        halved = -0.5 * inv
        p = [pf[i, at, :] for i in range(16)]
        t = tgt[at, :]
        total = [None] * 16
        for i in range(16):
            for j in range(i):
                e = p[i] - p[j]
                s = e * jnp.exp(e * e * halved)
                total[i] = s if total[i] is None else total[i] + s
                total[j] = -s if total[j] is None else total[j] - s
        scale = weight * inv
        for i in range(16):
            e = p[i] - t
            pf[i, at, :] = scale * (e * jnp.exp(e * e * halved) - total[i] * (1.0 / 16))
        return carry


    def gs_copy(v, r, share, back):
        return remote(
            ssend.at[r, pl.ds(48 * v, 48)],
            gs.at[pl.ds(48 * v, 48), share],
            gs_s.at[v, r],
            gs_r.at[v, r],
            mem=back,
        )

    for v in range(2):
        lax.fori_loop(6 * v, min(6 * v + 6, -(-VARS // 8)), scores, 0)

        def give_back(r, carry, v=v):
            ssend[r, 48 * v : 48 * v + 48, :] = pf[r, 48 * v : 48 * v + 48, :].astype(BF16)
            gs_copy(v, r, my_share, member(-r)).start()
            return carry

        lax.fori_loop(1, 16, give_back, 0)
        gs[48 * v : 48 * v + 48, my_share] = pf[0, 48 * v : 48 * v + 48, :].astype(BF16)

    def gs_wait(r, carry):
        share = pl.ds(pl.multiple_of(member(r) * 128, 128), 128)
        for v in range(2):
            gs_copy(v, r, share, member(r)).wait_recv()
        return carry

    lax.fori_loop(1, 16, gs_wait, 0)

    head = jnp.dot(gs[...], hidden[...], preferred_element_type=F32)
    for j in range(16):
        lo, left = 24 * (j // 4), 128 * (j % 4)
        hp[j] = head[lo : lo + 24, left : left + 128].astype(BF16)

    def hr_copy(r):
        return remote(hp.at[member(r)], hr.at[r], hr_s.at[r], hr_r.at[r], mem=member(r))

    def spread(r, carry):
        hr_copy(r).start()
        return carry

    lax.fori_loop(1, 16, spread, 0)
    hr[0] = hp[me_m]

    def grad_copy(j):
        at = pl.ds(pl.multiple_of(j * 512, 512), 512)
        return pltpu.make_async_copy(skipv.at[at], grad_out.at[at], grad_sem.at[j])

    def gradient(j, carry):
        at = pl.ds(pl.multiple_of(j * 512, 512), 512)
        skipv[at, :] = lax.dot_general(
            gs[:, at], wht[...], (((0,), (0,)), ((), ())), preferred_element_type=F32
        ).astype(BF16)
        grad_copy(j).start()
        return carry

    lax.fori_loop(0, 4, gradient, 0)

    def hr_wait(r, carry):
        hr_copy(r).wait_recv()
        return carry

    lax.fori_loop(1, 16, hr_wait, 0)
    summed = hr[0].astype(F32)
    for r in range(1, 16):
        summed = summed + hr[r].astype(F32)
    summed = (summed * (1.0 / math.sqrt(32768))).astype(BF16)
    hs[...] = summed
    hall[me_m] = summed

    def ha_copy(r, owner):
        return remote(hs, hall.at[owner], ha_s.at[r], ha_r.at[r], mem=member(r))

    def tell(r, carry):
        ha_copy(r, me_m).start()
        return carry

    lax.fori_loop(1, 16, tell, 0)

    for copy in row_copies + near[0] + near[1] + next_one + sib_copies:
        copy.wait_send()

    def far_done(j, carry):
        o = 2 - (j + 1) // 2
        even = lax.rem(j, 2)
        for h in range(2):
            for side in range(2):
                far_copy(h, side, j, o if side == 0 else -o, even if side == 0 else 1 - even)[
                    1
                ].wait_send()
        return carry

    lax.fori_loop(0, 3, far_done, 0)

    def members_done(r, carry):
        pred_copy(member(r))[1].wait_send()
        for v in range(2):
            gs_copy(v, r, my_share, member(-r)).wait_send()
        hr_copy(r).wait_send()
        return carry

    lax.fori_loop(1, 16, members_done, 0)

    def grad_done(j, carry):
        grad_copy(j).wait()
        return carry

    lax.fori_loop(0, 4, grad_done, 0)

    def ha_wait(r, carry):
        ha_copy(r, member(-r)).wait_recv()
        return carry

    lax.fori_loop(1, 16, ha_wait, 0)
    for j in range(16):
        lo = 24 * (j // 4)
        n = min(24, VARS - lo)
        head_out[lo : lo + n, 0, 128 * (j % 4) : 128 * (j % 4) + 128] = hall[j].astype(F32)[:n]


    def told(r, carry):
        ha_copy(r, me_m).wait_send()
        return carry

    lax.fori_loop(1, 16, told, 0)


def shards(
    coarse_latents,
    send_rows,
    up_index,
    up_weight,
    neighbors,
    live_counts,
    area,
    fine_skip,
    targets,
    kernel_width,
    w_in,
    w_out,
    ln_gain,
    w_head,
):
    hbm = pl.BlockSpec(memory_space=pl.ANY)
    vmem = pl.BlockSpec(memory_space=pltpu.VMEM)
    smem = pl.BlockSpec(memory_space=pltpu.SMEM)
    dma = pltpu.SemaphoreType.DMA
    grad_latent, head = pl.pallas_call(
        kernel,
        name="decoder_tail",
        out_shape=(
            jax.ShapeDtypeStruct((2048, 512), BF16),
            jax.ShapeDtypeStruct((VARS, 1, 512), F32),
        ),
        in_specs=[hbm] * 5 + [smem] + [hbm] * 8,
        out_specs=(hbm, vmem),
        scratch_shapes=[
            pltpu.VMEM((16, 128), jnp.int32),
            pltpu.VMEM((3, 2048), jnp.int32),
            pltpu.VMEM((3, 2048), F32),
            pltpu.VMEM((6, 2048), jnp.int32),
            pltpu.VMEM((1, 128), F32),
            pltpu.VMEM((VARS, 128), BF16),
            pltpu.VMEM((1, VARS), F32),
            pltpu.VMEM((1, 512), F32),
            pltpu.VMEM((VARS, 512), BF16),
            pltpu.VMEM((2, 5, 512, 256), BF16),
            pltpu.VMEM((4, 16, 128), jnp.int32),
            pltpu.VMEM((8, 2048, 512), BF16),
            pltpu.VMEM((2048, 512), BF16),
            pltpu.VMEM((6, 128, 128), F32),
            pltpu.VMEM((8, 256, 512), BF16),
            pltpu.VMEM((2, 2, 3, 128, 256), BF16),
            pltpu.VMEM((2, 5, 128, 256), BF16),
            pltpu.VMEM((2048, 512), F32),
            pltpu.VMEM((2048, 512), BF16),
            pltpu.VMEM((2304, 512), BF16),
            pltpu.VMEM((2048, 512), BF16),
            pltpu.VMEM((1024, 512), BF16),
            pltpu.VMEM((512, 512), BF16),
            pltpu.VMEM((VP, 512), BF16),
            pltpu.VMEM((8, 128), F32),
            pltpu.VMEM((VP, 128), F32),
            pltpu.VMEM((VP, 128), F32),
            pltpu.VMEM((16, VP, 128), BF16),
            pltpu.VMEM((16, VP, 128), BF16),
            pltpu.VMEM((16, VP, 128), F32),
            pltpu.VMEM((16, VP, 128), BF16),
            pltpu.VMEM((VP, 2048), BF16),
            pltpu.VMEM((16, 24, 128), BF16),
            pltpu.VMEM((16, 24, 128), BF16),
            pltpu.VMEM((24, 128), BF16),
            pltpu.VMEM((16, 24, 128), BF16),
            dma((14,)),
            dma((4,)),
            dma((2, 4)),
            dma((2, 4)),
            dma((4,)),
            dma((4,)),
            dma((2, 2, 3)),
            dma((2, 5)),
            dma((2, 8, 2)),
            dma((2,)),
            dma((2,)),
            dma((16,)),
            dma((16,)),
            dma((2, 16)),
            dma((2, 16)),
            dma((16,)),
            dma((16,)),
            dma((16,)),
            dma((16,)),
        ],
        compiler_params=pltpu.CompilerParams(
            collective_id=0, has_side_effects=True, vmem_limit_bytes=60 * 1024 * 1024
        ),
    )(
        coarse_latents[0],
        send_rows[0],
        up_index,
        up_weight,
        neighbors,
        live_counts,
        area[None],
        fine_skip,
        targets,
        kernel_width[None],
        w_in,
        w_out,
        ln_gain[None],
        w_head.T,
    )
    return grad_latent[None], head.transpose(1, 2, 0)


def solution(mesh):
    in_specs = (
        P("mem", "dom", None),
        P("dom", None, None),
        P(None, "dom"),
        P(None, "dom"),
        P(None, "dom"),
        P("dom"),
        P("dom"),
        P("dom", None),
        P(None, "dom"),
        P(),
        P(),
        P(),
        P(),
        P(),
    )
    out_specs = (P("mem", "dom", None), P("dom", None, None))
    return jax.shard_map(
        shards, mesh=mesh, in_specs=in_specs, out_specs=out_specs, check_vma=False
    )
```

```python
import functools
import math

import jax
import jax.numpy as jnp
from jax import lax
from jax.experimental import pallas as pl
from jax.experimental.pallas import tpu as pltpu
from jax.sharding import PartitionSpec as P

F32 = jnp.float32
BF16 = jnp.bfloat16
VARS = 83
VP = 96
NT = (((1,), (1,)), ((), ()))


def lanes_of(row):
    return jnp.broadcast_to(row, (128, 128)).T


def kernel(
    coarse,
    send_rows,
    up_index_h,
    up_weight_h,
    neighbors_h,
    live,
    area_h,
    skip,
    targets_h,
    kwidth_h,
    w_in,
    w_out,
    gain_h,
    w_head_h,
    grad_out,
    head_out,
    own_rows,
    up_index,
    up_weight,
    neighbors,
    area,
    targets,
    kwidth,
    gain,
    w_head,
    tiles,
    rows,
    wbuf,
    nbuf,
    cols,
    recv,
    sbuf,
    sibbuf,
    acc,
    skipv,
    ext,
    hidden,
    win,
    wout,
    wht,
    kwp,
    inv_b,
    tgt,
    psend,
    pall,
    pf,
    ssend,
    gs,
    hp,
    hr,
    hs,
    hall,
    loc_sem,
    grad_sem,
    tile_s,
    tile_r,
    rows_s,
    rows_r,
    g_s,
    sib_s,
    recv_sem,
    rim_s,
    rim_r,
    pred_s,
    pred_r,
    gs_s,
    gs_r,
    hr_s,
    hr_r,
    ha_s,
    ha_r,
):
    me_d = lax.axis_index("dom")
    me_m = lax.axis_index("mem")
    c = me_d // 2
    k = me_d - 2 * c
    other = 1 - k

    def chip(offset):
        return lax.rem(c + offset + 8, 8)

    def member(offset):
        return lax.rem(me_m + offset + 16, 16)

    def remote(src, dst, ssem, rsem, **device):
        return pltpu.make_async_remote_copy(
            src_ref=src,
            dst_ref=dst,
            send_sem=ssem,
            recv_sem=rsem,
            device_id=device,
            device_id_type=pl.DeviceIdType.MESH,
        )

    barrier = pltpu.get_barrier_semaphore()

    def greet(r, carry):
        pl.semaphore_signal(
            barrier,
            inc=1,
            device_id={"dom": lax.rem(me_d + r, 16)},
            device_id_type=pl.DeviceIdType.MESH,
        )
        pl.semaphore_signal(
            barrier, inc=1, device_id={"mem": member(r)}, device_id_type=pl.DeviceIdType.MESH
        )
        return carry

    lax.fori_loop(1, 16, greet, 0)
    my_share = pl.ds(pl.multiple_of(me_m * 128, 128), 128)
    loads = [
        pltpu.make_async_copy(src, dst, loc_sem.at[i])
        for i, (src, dst) in enumerate(
            (
                (send_rows, own_rows),
                (coarse.at[:, :256], tiles.at[0, 0]),
                (coarse.at[:, 256:], tiles.at[1, 0]),
                (neighbors_h, neighbors),
                (w_head_h, w_head),
                (kwidth_h, kwidth),
                (targets_h.at[:, my_share], targets),
                (area_h.at[:, my_share], area),
                (up_index_h, up_index),
                (up_weight_h, up_weight),
                (gain_h, gain),
                (skip, skipv),
                (w_in, win),
                (w_out, wout),
            )
        )
    ]
    pl.semaphore_wait(barrier, 30)

    next_to = (chip(1) * 2 + k, chip(-1) * 2 + k)

    def pass_on(h, src, slot, side):
        return remote(
            src,
            tiles.at[h, slot],
            tile_s.at[h, slot - 1],
            tile_r.at[h, slot - 1],
            dom=next_to[side],
        )

    def pass_rows(src, slot, side):
        return remote(
            src,
            rows.at[slot - 1],
            rows_s.at[slot - 1],
            rows_r.at[slot - 1],
            dom=next_to[side],
        )

    row_copies = [pass_rows(send_rows, 1 + side, side) for side in range(2)]
    near = [
        [
            pass_on(h, coarse.at[:, 256 * h : 256 * h + 256], 1 + side, side)
            for side in range(2)
        ]
        for h in range(2)
    ]
    for copy in row_copies + near[0] + near[1]:
        copy.start()
    for load in loads:
        load.start()

    lane = lax.broadcasted_iota(jnp.int32, (128, 128), 1).astype(F32)

    def picked(table, tile, dest):
        row = table[pl.ds(dest, 1), :].astype(F32)
        col = lanes_of(row)
        hot = jnp.concatenate(
            [jnp.where(col == lane + 128.0 * q, 1.0, 0.0).astype(BF16) for q in range(4)], axis=1
        )
        return jnp.dot(hot, tile[...], preferred_element_type=F32).astype(BF16)

    my_rows = pl.ds(pl.multiple_of(k * 128, 128), 128)

    def at_home(table, slot, rel):
        for h in range(2):
            tile = tiles.at[h, slot]
            lanes = slice(256 * h, 256 * h + 256)
            sibbuf[h, slot] = picked(table, tile, me_d + other - k)
            copy = remote(
                sibbuf.at[h, slot],
                recv.at[rel, my_rows, lanes],
                sib_s.at[h, slot],
                recv_sem.at[h, rel, k],
                dom=c * 2 + other,
            )
            copy.start()
            recv[rel, my_rows, lanes] = picked(table, tile, me_d)
            sib_copies.append(copy)

    sib_copies = []
    for load in loads[:3]:
        load.wait()
    at_home(own_rows, 0, 0)

    def weights_of(t, carry):
        at = pl.ds(pl.multiple_of(t * 128, 128), 128)
        for j in range(3):
            cols[j] = lanes_of(up_index[j : j + 1, at].astype(F32))
            cols[3 + j] = lanes_of(up_weight[j : j + 1, at])

        def part(s, carry):
            sub = pl.ds(pl.multiple_of(s * 32, 32), 32)
            out = pl.ds(pl.multiple_of(t * 128 + s * 32, 32), 32)
            idx = [cols[j, sub, :] for j in range(3)]
            wgt = [cols[3 + j, sub, :] for j in range(3)]
            base = lax.broadcasted_iota(jnp.int32, (32, 128), 1).astype(F32)
            for q in range(16):
                slot = base + 128.0 * q
                w = (
                    jnp.where(idx[0] == slot, wgt[0], 0.0)
                    + jnp.where(idx[1] == slot, wgt[1], 0.0)
                    + jnp.where(idx[2] == slot, wgt[2], 0.0)
                )
                hi = w.astype(BF16)
                lo = (w - hi.astype(F32)).astype(BF16)
                wbuf[q // 2, out, (q % 2) * 128 : (q % 2) * 128 + 128] = hi
                wbuf[q // 2, out, 256 + (q % 2) * 128 : 384 + (q % 2) * 128] = lo
            return carry

        lax.fori_loop(0, 4, part, 0)
        return carry

    def counts_of(t, carry):
        at = pl.ds(pl.multiple_of(t * 128, 128), 128)
        shift = ((t // 2) * 256).astype(F32)
        for j in range(6):
            cols[j] = lanes_of(neighbors[j : j + 1, at].astype(F32) - shift)

        def part(s, carry):
            sub = pl.ds(pl.multiple_of(s * 32, 32), 32)
            out = pl.ds(pl.multiple_of(t * 128 + s * 32, 32), 32)
            idx = [cols[j, sub, :] for j in range(6)]
            base = lax.broadcasted_iota(jnp.int32, (32, 128), 1).astype(F32)
            for q in range(4):
                spot = base + 128.0 * q
                total = jnp.where(idx[0] == spot, 1.0, 0.0)
                for j in range(1, 6):
                    total = total + jnp.where(idx[j] == spot, 1.0, 0.0)
                nbuf[out, q * 128 : q * 128 + 128] = total.astype(BF16)
            return carry

        lax.fori_loop(0, 4, part, 0)
        return carry

    for load in loads[3:8]:
        load.wait()
    wht[...] = jnp.zeros((VP, 512), BF16)
    wht[:VARS, :] = w_head[...]
    kwp[...] = jnp.ones((8, 128), F32)
    kwp[0:1, :VARS] = kwidth[...]
    width = kwp[0:1, :]
    inv_b[...] = lanes_of(1.0 / (width * width))[:VP]
    tgt[...] = jnp.zeros((VP, 128), F32)
    tgt[:VARS, :] = targets[...].astype(F32)

    lax.fori_loop(0, 16, counts_of, 0)

    for copy in row_copies:
        copy.wait_recv()
    row_copies += [pass_rows(rows.at[side], 3 + side, side) for side in range(2)]
    for copy in row_copies[2:]:
        copy.start()
    next_one = []

    def forward(h):
        for side in range(2):
            near[h][side].wait_recv()
            copy = pass_on(h, tiles.at[h, 1 + side], 3 + side, side)
            copy.start()
            next_one.append(copy)

    forward(0)
    for load in loads[8:10]:
        load.wait()
    lax.fori_loop(0, 8, weights_of, 0)
    forward(1)
    at_home(rows.at[0], 1, 7)
    at_home(rows.at[1], 2, 1)
    lax.fori_loop(8, 16, weights_of, 0)
    for load in loads[10:]:
        load.wait()

    def far_copy(h, side, j, o, kd):
        dest = chip(o) * 2 + kd
        rel = 5 - j // 2 if side == 0 else 3 + j // 2
        return dest, remote(
            sbuf.at[h, side, j],
            recv.at[rel, my_rows, 256 * h : 256 * h + 256],
            g_s.at[h, side, j],
            recv_sem.at[h, rel, k],
            dom=dest,
        )

    def send_far(h):
        for copy in next_one[2 * h : 2 * h + 2]:
            copy.wait_recv()

        def both_ways(j, carry):
            o = 1 + j // 2
            even = lax.rem(j, 2)
            for side in range(2):
                dest, copy = far_copy(
                    h, side, j, o if side == 0 else -o, even if side == 0 else 1 - even
                )
                sbuf[h, side, j] = picked(rows.at[2 + side], tiles.at[h, 3 + side], dest)
                copy.start()
            return carry

        lax.fori_loop(0, 3, both_ways, 0)

    def arrived(rel, kb):
        half = pl.ds(pl.multiple_of(kb * 128, 128), 128)
        for h in range(2):
            remote(
                sibbuf.at[h, 0],
                recv.at[rel, half, 256 * h : 256 * h + 256],
                sib_s.at[h, 0],
                recv_sem.at[h, rel, kb],
                dom=c * 2 + other,
            ).wait_recv()

    def added(rels, t):
        at = pl.ds(pl.multiple_of(t * 512, 512), 512)
        total = skipv[at, :].astype(F32) if rels[0] == 0 else acc[at, :]
        for rel in rels:
            here = chip(rel)
            table = recv[rel]
            total = total + jnp.dot(wbuf[here, at, :256], table, preferred_element_type=F32)
            total = total + jnp.dot(wbuf[here, at, 256:], table, preferred_element_type=F32)
        return at, total

    def unpool(rels):
        for rel in rels:
            arrived(rel, other)
            if rel in (3, 4, 5):
                arrived(rel, k)

        def accumulate(t, carry, rels=rels):
            at, total = added(rels, t)
            acc[at, :] = total
            return carry

        lax.fori_loop(0, 4, accumulate, 0)

    for copy in row_copies[2:]:
        copy.wait_recv()
    send_far(0)
    unpool((0,))
    unpool((7, 1))
    send_far(1)
    at_home(rows.at[2], 3, 6)
    at_home(rows.at[3], 4, 2)
    unpool((6, 2))
    unpool((5, 3))
    arrived(4, 0)
    arrived(4, 1)

    def finish(t, carry):
        total = added((4,), t)[1]
        ext[pl.ds(pl.multiple_of(t * 512 + 128, 128), 512), :] = total.astype(BF16)
        return carry

    lax.fori_loop(0, 2, lambda t, carry: finish(t * 3, carry), 0)
    rims = [
        remote(
            ext.at[pl.ds(2048, 128)],
            ext.at[pl.ds(0, 128)],
            rim_s.at[0],
            rim_r.at[0],
            dom=lax.rem(me_d + 1, 16),
        ),
        remote(
            ext.at[pl.ds(128, 128)],
            ext.at[pl.ds(2176, 128)],
            rim_s.at[1],
            rim_r.at[1],
            dom=lax.rem(me_d + 15, 16),
        ),
    ]
    for rim in rims:
        rim.start()
    lax.fori_loop(1, 3, finish, 0)

    gain_row = gain[...]

    def pred_copy(j):
        r = lax.rem(j - me_m + 16, 16)
        return r, remote(psend.at[j], pall.at[r], pred_s.at[r], pred_r.at[r], mem=j)

    def dense(i, carry):
        x = ext[pl.ds(pl.multiple_of(i * 512 + 128, 128), 512), :]
        parts = []
        for s in range(2):
            start = pl.multiple_of(i * 512 + s * 256, 256)
            total = jnp.dot(
                nbuf[pl.ds(start, 256), :], ext[pl.ds(start, 512), :], preferred_element_type=F32
            )
            parts.append((total * (1.0 / 6)).astype(BF16))
        agg = jnp.concatenate(parts, axis=0)
        pre = jnp.dot(x, win[:512], preferred_element_type=F32) + jnp.dot(
            agg, win[512:], preferred_element_type=F32
        )
        half = 0.5 * pre
        act = (half + half * jnp.tanh(half)).astype(BF16)
        upd = jnp.dot(act, wout[...], preferred_element_type=F32)
        mean = jnp.sum(upd, axis=1, keepdims=True) * (1.0 / 512)
        centred = upd - mean
        var = jnp.sum(centred * centred, axis=1, keepdims=True) * (1.0 / 512)
        h = (x.astype(F32) + centred * lax.rsqrt(var + 1e-05) * gain_row).astype(BF16)
        hidden[pl.ds(pl.multiple_of(i * 512, 512), 512), :] = h
        pred = lax.dot_general(wht[...], h, NT, preferred_element_type=F32).astype(BF16)
        for s in range(4):
            j = 4 * i + s
            r, copy = pred_copy(j)
            psend[j] = pred[:, s * 128 : s * 128 + 128]

            @pl.when(r != 0)
            def _():
                copy.start()

            @pl.when(r == 0)
            def _():
                pall[0] = psend[j]

        return carry

    lax.fori_loop(1, 3, dense, 0)
    for rim in rims:
        rim.wait()

    @pl.when(me_d == 0)
    def _():
        ext[pl.ds(0, 128), :] = jnp.zeros((128, 512), BF16)

    @pl.when(me_d == 15)
    def _():
        ext[pl.ds(2176, 128), :] = jnp.zeros((128, 512), BF16)

    lax.fori_loop(0, 2, lambda t, carry: dense(t * 3, carry), 0)

    def pred_wait(r, carry):
        remote(psend.at[0], pall.at[r], pred_s.at[r], pred_r.at[r], mem=member(r)).wait_recv()
        return carry

    lax.fori_loop(1, 16, pred_wait, 0)

    def widen(r, carry):
        pf[r] = pall[r].astype(F32)
        return carry

    lax.fori_loop(0, 16, widen, 0)
    place = lax.broadcasted_iota(jnp.int32, (1, 128), 1) + me_m * 128
    weight = jnp.broadcast_to(jnp.where(place < live[0], area[...], 0.0), (8, 128))

    def scores(q, carry):
        at = pl.ds(pl.multiple_of(q * 8, 8), 8)
        inv = inv_b[at, :]
        halved = -0.5 * inv
        p = [pf[i, at, :] for i in range(16)]
        t = tgt[at, :]
        total = [None] * 16
        for i in range(16):
            for j in range(i):
                e = p[i] - p[j]
                s = e * jnp.exp(e * e * halved)
                total[i] = s if total[i] is None else total[i] + s
                total[j] = -s if total[j] is None else total[j] - s
        scale = weight * inv
        for i in range(16):
            e = p[i] - t
            pf[i, at, :] = scale * (e * jnp.exp(e * e * halved) - total[i] * (1.0 / 16))
        return carry


    def gs_copy(v, r, share, back):
        return remote(
            ssend.at[r, pl.ds(48 * v, 48)],
            gs.at[pl.ds(48 * v, 48), share],
            gs_s.at[v, r],
            gs_r.at[v, r],
            mem=back,
        )

    for v in range(2):
        lax.fori_loop(6 * v, min(6 * v + 6, -(-VARS // 8)), scores, 0)

        def give_back(r, carry, v=v):
            ssend[r, 48 * v : 48 * v + 48, :] = pf[r, 48 * v : 48 * v + 48, :].astype(BF16)
            gs_copy(v, r, my_share, member(-r)).start()
            return carry

        lax.fori_loop(1, 16, give_back, 0)
        gs[48 * v : 48 * v + 48, my_share] = pf[0, 48 * v : 48 * v + 48, :].astype(BF16)

    def gs_wait(r, carry):
        share = pl.ds(pl.multiple_of(member(r) * 128, 128), 128)
        for v in range(2):
            gs_copy(v, r, share, member(r)).wait_recv()
        return carry

    lax.fori_loop(1, 16, gs_wait, 0)

    head = jnp.dot(gs[...], hidden[...], preferred_element_type=F32)
    for j in range(16):
        lo, left = 24 * (j // 4), 128 * (j % 4)
        hp[j] = head[lo : lo + 24, left : left + 128].astype(BF16)

    def hr_copy(r):
        return remote(hp.at[member(r)], hr.at[r], hr_s.at[r], hr_r.at[r], mem=member(r))

    def spread(r, carry):
        hr_copy(r).start()
        return carry

    lax.fori_loop(1, 16, spread, 0)
    hr[0] = hp[me_m]

    def grad_copy(j):
        at = pl.ds(pl.multiple_of(j * 512, 512), 512)
        return pltpu.make_async_copy(skipv.at[at], grad_out.at[at], grad_sem.at[j])

    def gradient(j, carry):
        at = pl.ds(pl.multiple_of(j * 512, 512), 512)
        skipv[at, :] = lax.dot_general(
            gs[:, at], wht[...], (((0,), (0,)), ((), ())), preferred_element_type=F32
        ).astype(BF16)
        grad_copy(j).start()
        return carry

    lax.fori_loop(0, 4, gradient, 0)

    def hr_wait(r, carry):
        hr_copy(r).wait_recv()
        return carry

    lax.fori_loop(1, 16, hr_wait, 0)
    summed = hr[0].astype(F32)
    for r in range(1, 16):
        summed = summed + hr[r].astype(F32)
    summed = (summed * (1.0 / math.sqrt(32768))).astype(BF16)
    hs[...] = summed
    hall[me_m] = summed

    def ha_copy(r, owner):
        return remote(hs, hall.at[owner], ha_s.at[r], ha_r.at[r], mem=member(r))

    def tell(r, carry):
        ha_copy(r, me_m).start()
        return carry

    lax.fori_loop(1, 16, tell, 0)

    for copy in row_copies + near[0] + near[1] + next_one + sib_copies:
        copy.wait_send()

    def far_done(j, carry):
        o = 1 + j // 2
        even = lax.rem(j, 2)
        for h in range(2):
            for side in range(2):
                far_copy(h, side, j, o if side == 0 else -o, even if side == 0 else 1 - even)[
                    1
                ].wait_send()
        return carry

    lax.fori_loop(0, 3, far_done, 0)

    def members_done(r, carry):
        pred_copy(member(r))[1].wait_send()
        for v in range(2):
            gs_copy(v, r, my_share, member(-r)).wait_send()
        hr_copy(r).wait_send()
        return carry

    lax.fori_loop(1, 16, members_done, 0)

    def grad_done(j, carry):
        grad_copy(j).wait()
        return carry

    lax.fori_loop(0, 4, grad_done, 0)

    def ha_wait(r, carry):
        ha_copy(r, member(-r)).wait_recv()
        return carry

    lax.fori_loop(1, 16, ha_wait, 0)
    for j in range(16):
        lo = 24 * (j // 4)
        n = min(24, VARS - lo)
        head_out[lo : lo + n, 0, 128 * (j % 4) : 128 * (j % 4) + 128] = hall[j].astype(F32)[:n]


    def told(r, carry):
        ha_copy(r, me_m).wait_send()
        return carry

    lax.fori_loop(1, 16, told, 0)


def shards(
    coarse_latents,
    send_rows,
    up_index,
    up_weight,
    neighbors,
    live_counts,
    area,
    fine_skip,
    targets,
    kernel_width,
    w_in,
    w_out,
    ln_gain,
    w_head,
):
    hbm = pl.BlockSpec(memory_space=pl.ANY)
    vmem = pl.BlockSpec(memory_space=pltpu.VMEM)
    smem = pl.BlockSpec(memory_space=pltpu.SMEM)
    dma = pltpu.SemaphoreType.DMA
    grad_latent, head = pl.pallas_call(
        kernel,
        name="decoder_tail",
        out_shape=(
            jax.ShapeDtypeStruct((2048, 512), BF16),
            jax.ShapeDtypeStruct((VARS, 1, 512), F32),
        ),
        in_specs=[hbm] * 5 + [smem] + [hbm] * 8,
        out_specs=(hbm, vmem),
        scratch_shapes=[
            pltpu.VMEM((16, 128), jnp.int32),
            pltpu.VMEM((3, 2048), jnp.int32),
            pltpu.VMEM((3, 2048), F32),
            pltpu.VMEM((6, 2048), jnp.int32),
            pltpu.VMEM((1, 128), F32),
            pltpu.VMEM((VARS, 128), BF16),
            pltpu.VMEM((1, VARS), F32),
            pltpu.VMEM((1, 512), F32),
            pltpu.VMEM((VARS, 512), BF16),
            pltpu.VMEM((2, 5, 512, 256), BF16),
            pltpu.VMEM((4, 16, 128), jnp.int32),
            pltpu.VMEM((8, 2048, 512), BF16),
            pltpu.VMEM((2048, 512), BF16),
            pltpu.VMEM((6, 128, 128), F32),
            pltpu.VMEM((8, 256, 512), BF16),
            pltpu.VMEM((2, 2, 3, 128, 256), BF16),
            pltpu.VMEM((2, 5, 128, 256), BF16),
            pltpu.VMEM((2048, 512), F32),
            pltpu.VMEM((2048, 512), BF16),
            pltpu.VMEM((2304, 512), BF16),
            pltpu.VMEM((2048, 512), BF16),
            pltpu.VMEM((1024, 512), BF16),
            pltpu.VMEM((512, 512), BF16),
            pltpu.VMEM((VP, 512), BF16),
            pltpu.VMEM((8, 128), F32),
            pltpu.VMEM((VP, 128), F32),
            pltpu.VMEM((VP, 128), F32),
            pltpu.VMEM((16, VP, 128), BF16),
            pltpu.VMEM((16, VP, 128), BF16),
            pltpu.VMEM((16, VP, 128), F32),
            pltpu.VMEM((16, VP, 128), BF16),
            pltpu.VMEM((VP, 2048), BF16),
            pltpu.VMEM((16, 24, 128), BF16),
            pltpu.VMEM((16, 24, 128), BF16),
            pltpu.VMEM((24, 128), BF16),
            pltpu.VMEM((16, 24, 128), BF16),
            dma((14,)),
            dma((4,)),
            dma((2, 4)),
            dma((2, 4)),
            dma((4,)),
            dma((4,)),
            dma((2, 2, 3)),
            dma((2, 5)),
            dma((2, 8, 2)),
            dma((2,)),
            dma((2,)),
            dma((16,)),
            dma((16,)),
            dma((2, 16)),
            dma((2, 16)),
            dma((16,)),
            dma((16,)),
            dma((16,)),
            dma((16,)),
        ],
        compiler_params=pltpu.CompilerParams(
            collective_id=0, has_side_effects=True, vmem_limit_bytes=60 * 1024 * 1024
        ),
    )(
        coarse_latents[0],
        send_rows[0],
        up_index,
        up_weight,
        neighbors,
        live_counts,
        area[None],
        fine_skip,
        targets,
        kernel_width[None],
        w_in,
        w_out,
        ln_gain[None],
        w_head.T,
    )
    return grad_latent[None], head.transpose(1, 2, 0)


def solution(mesh):
    in_specs = (
        P("mem", "dom", None),
        P("dom", None, None),
        P(None, "dom"),
        P(None, "dom"),
        P(None, "dom"),
        P("dom"),
        P("dom"),
        P("dom", None),
        P(None, "dom"),
        P(),
        P(),
        P(),
        P(),
        P(),
    )
    out_specs = (P("mem", "dom", None), P("dom", None, None))
    return jax.shard_map(
        shards, mesh=mesh, in_specs=in_specs, out_specs=out_specs, check_vma=False
    )
```

```python
import functools
import math

import jax
import jax.numpy as jnp
from jax import lax
from jax.experimental import pallas as pl
from jax.experimental.pallas import tpu as pltpu
from jax.sharding import PartitionSpec as P

F32 = jnp.float32
BF16 = jnp.bfloat16
VARS = 83
VP = 96
NT = (((1,), (1,)), ((), ()))


def lanes_of(row):
    return jnp.broadcast_to(row, (128, 128)).T


def kernel(
    coarse,
    send_rows,
    up_index_h,
    up_weight_h,
    neighbors_h,
    live,
    area_h,
    skip,
    targets_h,
    kwidth_h,
    w_in,
    w_out,
    gain_h,
    w_head_h,
    grad_out,
    head_out,
    own_rows,
    up_index,
    up_weight,
    neighbors,
    area,
    targets,
    kwidth,
    gain,
    w_head,
    tiles,
    rows,
    wbuf,
    nbuf,
    cols,
    recv,
    sbuf,
    sibbuf,
    acc,
    skipv,
    ext,
    hidden,
    win,
    wout,
    wht,
    kwp,
    inv_b,
    tgt,
    psend,
    pall,
    pf,
    ssend,
    gs,
    hp,
    hr,
    hs,
    hall,
    word,
    loc_sem,
    grad_sem,
    tile_s,
    tile_r,
    rows_s,
    rows_r,
    g_s,
    sib_s,
    recv_sem,
    rim_s,
    rim_r,
    pred_s,
    pred_r,
    gs_s,
    gs_r,
    hr_s,
    hr_r,
    ha_s,
    ha_r,
):
    me_d = lax.axis_index("dom")
    me_m = lax.axis_index("mem")
    c = me_d // 2
    k = me_d - 2 * c
    other = 1 - k

    def chip(offset):
        return lax.rem(c + offset + 8, 8)

    def member(offset):
        return lax.rem(me_m + offset + 16, 16)

    def remote(src, dst, ssem, rsem, **device):
        return pltpu.make_async_remote_copy(
            src_ref=src,
            dst_ref=dst,
            send_sem=ssem,
            recv_sem=rsem,
            device_id=device,
            device_id_type=pl.DeviceIdType.MESH,
        )

    barrier = pltpu.get_barrier_semaphore()

    east = lax.rem(me_m, 4)
    north = me_m // 4
    z_ring = [{"dom": chip(step) * 2 + k} for step in (1, -1)]
    x_ring = [{"mem": north * 4 + lax.rem(east + step, 4)} for step in (1, 3)]
    y_ring = [{"mem": lax.rem(north + step, 4) * 4 + east} for step in (1, 3)]
    pair = [{"dom": c * 2 + other}]

    def greet(sem, devices):
        for device in devices:
            pl.semaphore_signal(
                sem, inc=1, device_id=device, device_id_type=pl.DeviceIdType.MESH
            )

    rounds = (z_ring, z_ring, z_ring, pair, x_ring, y_ring, y_ring)

    def heard(i):
        pl.semaphore_wait(word.at[i], len(rounds[i]))
        if i + 1 < len(rounds):
            greet(word.at[i + 1], rounds[i + 1])

    greet(barrier, z_ring + pair + x_ring + y_ring)
    my_share = pl.ds(pl.multiple_of(me_m * 128, 128), 128)
    loads = [
        pltpu.make_async_copy(src, dst, loc_sem.at[i])
        for i, (src, dst) in enumerate(
            (
                (send_rows, own_rows),
                (coarse.at[:, :256], tiles.at[0, 0]),
                (coarse.at[:, 256:], tiles.at[1, 0]),
                (neighbors_h, neighbors),
                (w_head_h, w_head),
                (kwidth_h, kwidth),
                (targets_h.at[:, my_share], targets),
                (area_h.at[:, my_share], area),
                (up_index_h, up_index),
                (up_weight_h, up_weight),
                (gain_h, gain),
                (skip, skipv),
                (w_in, win),
                (w_out, wout),
            )
        )
    ]
    pl.semaphore_wait(barrier, 7)

    next_to = (chip(1) * 2 + k, chip(-1) * 2 + k)

    def pass_on(h, src, slot, side):
        return remote(
            src,
            tiles.at[h, slot],
            tile_s.at[h, slot - 1],
            tile_r.at[h, slot - 1],
            dom=next_to[side],
        )

    def pass_rows(src, slot, side):
        return remote(
            src,
            rows.at[slot - 1],
            rows_s.at[slot - 1],
            rows_r.at[slot - 1],
            dom=next_to[side],
        )

    row_copies = [pass_rows(send_rows, 1 + side, side) for side in range(2)]
    near = [
        [
            pass_on(h, coarse.at[:, 256 * h : 256 * h + 256], 1 + side, side)
            for side in range(2)
        ]
        for h in range(2)
    ]
    for copy in row_copies + near[0] + near[1]:
        copy.start()
    greet(word.at[0], rounds[0])
    for load in loads:
        load.start()

    lane = lax.broadcasted_iota(jnp.int32, (128, 128), 1).astype(F32)

    def picked(table, tile, dest):
        row = table[pl.ds(dest, 1), :].astype(F32)
        col = lanes_of(row)
        hot = jnp.concatenate(
            [jnp.where(col == lane + 128.0 * q, 1.0, 0.0).astype(BF16) for q in range(4)], axis=1
        )
        return jnp.dot(hot, tile[...], preferred_element_type=F32).astype(BF16)

    my_rows = pl.ds(pl.multiple_of(k * 128, 128), 128)

    def at_home(table, slot, rel):
        for h in range(2):
            tile = tiles.at[h, slot]
            lanes = slice(256 * h, 256 * h + 256)
            sibbuf[h, slot] = picked(table, tile, me_d + other - k)
            copy = remote(
                sibbuf.at[h, slot],
                recv.at[rel, my_rows, lanes],
                sib_s.at[h, slot],
                recv_sem.at[h, rel, k],
                dom=c * 2 + other,
            )
            copy.start()
            recv[rel, my_rows, lanes] = picked(table, tile, me_d)
            sib_copies.append(copy)

    sib_copies = []
    for load in loads[:3]:
        load.wait()
    at_home(own_rows, 0, 0)
    heard(0)

    def weights_of(t, carry):
        at = pl.ds(pl.multiple_of(t * 128, 128), 128)
        for j in range(3):
            cols[j] = lanes_of(up_index[j : j + 1, at].astype(F32))
            cols[3 + j] = lanes_of(up_weight[j : j + 1, at])

        def part(s, carry):
            sub = pl.ds(pl.multiple_of(s * 32, 32), 32)
            out = pl.ds(pl.multiple_of(t * 128 + s * 32, 32), 32)
            idx = [cols[j, sub, :] for j in range(3)]
            wgt = [cols[3 + j, sub, :] for j in range(3)]
            base = lax.broadcasted_iota(jnp.int32, (32, 128), 1).astype(F32)
            for q in range(16):
                slot = base + 128.0 * q
                w = (
                    jnp.where(idx[0] == slot, wgt[0], 0.0)
                    + jnp.where(idx[1] == slot, wgt[1], 0.0)
                    + jnp.where(idx[2] == slot, wgt[2], 0.0)
                )
                hi = w.astype(BF16)
                lo = (w - hi.astype(F32)).astype(BF16)
                wbuf[q // 2, out, (q % 2) * 128 : (q % 2) * 128 + 128] = hi
                wbuf[q // 2, out, 256 + (q % 2) * 128 : 384 + (q % 2) * 128] = lo
            return carry

        lax.fori_loop(0, 4, part, 0)
        return carry

    def counts_of(t, carry):
        at = pl.ds(pl.multiple_of(t * 128, 128), 128)
        shift = ((t // 2) * 256).astype(F32)
        for j in range(6):
            cols[j] = lanes_of(neighbors[j : j + 1, at].astype(F32) - shift)

        def part(s, carry):
            sub = pl.ds(pl.multiple_of(s * 32, 32), 32)
            out = pl.ds(pl.multiple_of(t * 128 + s * 32, 32), 32)
            idx = [cols[j, sub, :] for j in range(6)]
            base = lax.broadcasted_iota(jnp.int32, (32, 128), 1).astype(F32)
            for q in range(4):
                spot = base + 128.0 * q
                total = jnp.where(idx[0] == spot, 1.0, 0.0)
                for j in range(1, 6):
                    total = total + jnp.where(idx[j] == spot, 1.0, 0.0)
                nbuf[out, q * 128 : q * 128 + 128] = total.astype(BF16)
            return carry

        lax.fori_loop(0, 4, part, 0)
        return carry

    for load in loads[3:8]:
        load.wait()
    wht[...] = jnp.zeros((VP, 512), BF16)
    wht[:VARS, :] = w_head[...]
    kwp[...] = jnp.ones((8, 128), F32)
    kwp[0:1, :VARS] = kwidth[...]
    width = kwp[0:1, :]
    inv_b[...] = lanes_of(1.0 / (width * width))[:VP]
    tgt[...] = jnp.zeros((VP, 128), F32)
    tgt[:VARS, :] = targets[...].astype(F32)

    heard(1)
    lax.fori_loop(0, 16, counts_of, 0)
    heard(2)

    for copy in row_copies:
        copy.wait_recv()
    row_copies += [pass_rows(rows.at[side], 3 + side, side) for side in range(2)]
    for copy in row_copies[2:]:
        copy.start()
    next_one = []

    def forward(h):
        for side in range(2):
            near[h][side].wait_recv()
            copy = pass_on(h, tiles.at[h, 1 + side], 3 + side, side)
            copy.start()
            next_one.append(copy)

    forward(0)
    for load in loads[8:10]:
        load.wait()
    lax.fori_loop(0, 8, weights_of, 0)
    heard(3)
    heard(4)
    forward(1)
    at_home(rows.at[0], 1, 7)
    at_home(rows.at[1], 2, 1)
    lax.fori_loop(8, 16, weights_of, 0)
    heard(5)
    heard(6)
    for load in loads[10:]:
        load.wait()

    def far_copy(h, side, j, o, kd):
        dest = chip(o) * 2 + kd
        rel = 5 - j // 2 if side == 0 else 3 + j // 2
        return dest, remote(
            sbuf.at[h, side, j],
            recv.at[rel, my_rows, 256 * h : 256 * h + 256],
            g_s.at[h, side, j],
            recv_sem.at[h, rel, k],
            dom=dest,
        )

    def send_far(h):
        for copy in next_one[2 * h : 2 * h + 2]:
            copy.wait_recv()

        def both_ways(j, carry):
            o = 1 + j // 2
            even = lax.rem(j, 2)
            for side in range(2):
                dest, copy = far_copy(
                    h, side, j, o if side == 0 else -o, even if side == 0 else 1 - even
                )
                sbuf[h, side, j] = picked(rows.at[2 + side], tiles.at[h, 3 + side], dest)
                copy.start()
            return carry

        lax.fori_loop(0, 3, both_ways, 0)

    def arrived(rel, kb):
        half = pl.ds(pl.multiple_of(kb * 128, 128), 128)
        for h in range(2):
            remote(
                sibbuf.at[h, 0],
                recv.at[rel, half, 256 * h : 256 * h + 256],
                sib_s.at[h, 0],
                recv_sem.at[h, rel, kb],
                dom=c * 2 + other,
            ).wait_recv()

    def added(rels, t):
        at = pl.ds(pl.multiple_of(t * 512, 512), 512)
        total = skipv[at, :].astype(F32) if rels[0] == 0 else acc[at, :]
        for rel in rels:
            here = chip(rel)
            table = recv[rel]
            total = total + jnp.dot(wbuf[here, at, :256], table, preferred_element_type=F32)
            total = total + jnp.dot(wbuf[here, at, 256:], table, preferred_element_type=F32)
        return at, total

    def unpool(rels):
        for rel in rels:
            arrived(rel, other)
            if rel in (3, 4, 5):
                arrived(rel, k)

        def accumulate(t, carry, rels=rels):
            at, total = added(rels, t)
            acc[at, :] = total
            return carry

        lax.fori_loop(0, 4, accumulate, 0)

    for copy in row_copies[2:]:
        copy.wait_recv()
    send_far(0)
    unpool((0,))
    unpool((7, 1))
    send_far(1)
    at_home(rows.at[2], 3, 6)
    at_home(rows.at[3], 4, 2)
    unpool((6, 2))
    unpool((5, 3))
    arrived(4, 0)
    arrived(4, 1)

    def finish(t, carry):
        total = added((4,), t)[1]
        ext[pl.ds(pl.multiple_of(t * 512 + 128, 128), 512), :] = total.astype(BF16)
        return carry

    lax.fori_loop(0, 2, lambda t, carry: finish(t * 3, carry), 0)
    rims = [
        remote(
            ext.at[pl.ds(2048, 128)],
            ext.at[pl.ds(0, 128)],
            rim_s.at[0],
            rim_r.at[0],
            dom=lax.rem(me_d + 1, 16),
        ),
        remote(
            ext.at[pl.ds(128, 128)],
            ext.at[pl.ds(2176, 128)],
            rim_s.at[1],
            rim_r.at[1],
            dom=lax.rem(me_d + 15, 16),
        ),
    ]
    for rim in rims:
        rim.start()
    lax.fori_loop(1, 3, finish, 0)

    gain_row = gain[...]

    def pred_copy(j):
        r = lax.rem(j - me_m + 16, 16)
        return r, remote(psend.at[j], pall.at[r], pred_s.at[r], pred_r.at[r], mem=j)

    def dense(i, carry):
        x = ext[pl.ds(pl.multiple_of(i * 512 + 128, 128), 512), :]
        parts = []
        for s in range(2):
            start = pl.multiple_of(i * 512 + s * 256, 256)
            total = jnp.dot(
                nbuf[pl.ds(start, 256), :], ext[pl.ds(start, 512), :], preferred_element_type=F32
            )
            parts.append((total * (1.0 / 6)).astype(BF16))
        agg = jnp.concatenate(parts, axis=0)
        pre = jnp.dot(x, win[:512], preferred_element_type=F32) + jnp.dot(
            agg, win[512:], preferred_element_type=F32
        )
        half = 0.5 * pre
        act = (half + half * jnp.tanh(half)).astype(BF16)
        upd = jnp.dot(act, wout[...], preferred_element_type=F32)
        mean = jnp.sum(upd, axis=1, keepdims=True) * (1.0 / 512)
        centred = upd - mean
        var = jnp.sum(centred * centred, axis=1, keepdims=True) * (1.0 / 512)
        h = (x.astype(F32) + centred * lax.rsqrt(var + 1e-05) * gain_row).astype(BF16)
        hidden[pl.ds(pl.multiple_of(i * 512, 512), 512), :] = h
        pred = lax.dot_general(wht[...], h, NT, preferred_element_type=F32).astype(BF16)
        for s in range(4):
            j = 4 * i + s
            r, copy = pred_copy(j)
            psend[j] = pred[:, s * 128 : s * 128 + 128]

            @pl.when(r != 0)
            def _():
                copy.start()

            @pl.when(r == 0)
            def _():
                pall[0] = psend[j]

        return carry

    lax.fori_loop(1, 3, dense, 0)
    for rim in rims:
        rim.wait()

    @pl.when(me_d == 0)
    def _():
        ext[pl.ds(0, 128), :] = jnp.zeros((128, 512), BF16)

    @pl.when(me_d == 15)
    def _():
        ext[pl.ds(2176, 128), :] = jnp.zeros((128, 512), BF16)

    lax.fori_loop(0, 2, lambda t, carry: dense(t * 3, carry), 0)

    def pred_wait(r, carry):
        remote(psend.at[0], pall.at[r], pred_s.at[r], pred_r.at[r], mem=member(r)).wait_recv()
        return carry

    lax.fori_loop(1, 16, pred_wait, 0)

    def widen(r, carry):
        pf[r] = pall[r].astype(F32)
        return carry

    lax.fori_loop(0, 16, widen, 0)
    place = lax.broadcasted_iota(jnp.int32, (1, 128), 1) + me_m * 128
    weight = jnp.broadcast_to(jnp.where(place < live[0], area[...], 0.0), (8, 128))

    def scores(q, carry):
        at = pl.ds(pl.multiple_of(q * 8, 8), 8)
        inv = inv_b[at, :]
        halved = -0.5 * inv
        p = [pf[i, at, :] for i in range(16)]
        t = tgt[at, :]
        total = [None] * 16
        for i in range(16):
            for j in range(i):
                e = p[i] - p[j]
                s = e * jnp.exp(e * e * halved)
                total[i] = s if total[i] is None else total[i] + s
                total[j] = -s if total[j] is None else total[j] - s
        scale = weight * inv
        for i in range(16):
            e = p[i] - t
            pf[i, at, :] = scale * (e * jnp.exp(e * e * halved) - total[i] * (1.0 / 16))
        return carry


    def gs_copy(v, r, share, back):
        return remote(
            ssend.at[r, pl.ds(48 * v, 48)],
            gs.at[pl.ds(48 * v, 48), share],
            gs_s.at[v, r],
            gs_r.at[v, r],
            mem=back,
        )

    for v in range(2):
        lax.fori_loop(6 * v, min(6 * v + 6, -(-VARS // 8)), scores, 0)

        def give_back(r, carry, v=v):
            ssend[r, 48 * v : 48 * v + 48, :] = pf[r, 48 * v : 48 * v + 48, :].astype(BF16)
            gs_copy(v, r, my_share, member(-r)).start()
            return carry

        lax.fori_loop(1, 16, give_back, 0)
        gs[48 * v : 48 * v + 48, my_share] = pf[0, 48 * v : 48 * v + 48, :].astype(BF16)

    def gs_wait(r, carry):
        share = pl.ds(pl.multiple_of(member(r) * 128, 128), 128)
        for v in range(2):
            gs_copy(v, r, share, member(r)).wait_recv()
        return carry

    lax.fori_loop(1, 16, gs_wait, 0)

    head = jnp.dot(gs[...], hidden[...], preferred_element_type=F32)
    for j in range(16):
        lo, left = 24 * (j // 4), 128 * (j % 4)
        hp[j] = head[lo : lo + 24, left : left + 128].astype(BF16)

    def hr_copy(r):
        return remote(hp.at[member(r)], hr.at[r], hr_s.at[r], hr_r.at[r], mem=member(r))

    def spread(r, carry):
        hr_copy(r).start()
        return carry

    lax.fori_loop(1, 16, spread, 0)
    hr[0] = hp[me_m]

    def grad_copy(j):
        at = pl.ds(pl.multiple_of(j * 512, 512), 512)
        return pltpu.make_async_copy(skipv.at[at], grad_out.at[at], grad_sem.at[j])

    def gradient(j, carry):
        at = pl.ds(pl.multiple_of(j * 512, 512), 512)
        skipv[at, :] = lax.dot_general(
            gs[:, at], wht[...], (((0,), (0,)), ((), ())), preferred_element_type=F32
        ).astype(BF16)
        grad_copy(j).start()
        return carry

    lax.fori_loop(0, 4, gradient, 0)

    def hr_wait(r, carry):
        hr_copy(r).wait_recv()
        return carry

    lax.fori_loop(1, 16, hr_wait, 0)
    summed = hr[0].astype(F32)
    for r in range(1, 16):
        summed = summed + hr[r].astype(F32)
    summed = (summed * (1.0 / math.sqrt(32768))).astype(BF16)
    hs[...] = summed
    hall[me_m] = summed

    def ha_copy(r, owner):
        return remote(hs, hall.at[owner], ha_s.at[r], ha_r.at[r], mem=member(r))

    def tell(r, carry):
        ha_copy(r, me_m).start()
        return carry

    lax.fori_loop(1, 16, tell, 0)

    for copy in row_copies + near[0] + near[1] + next_one + sib_copies:
        copy.wait_send()

    def far_done(j, carry):
        o = 1 + j // 2
        even = lax.rem(j, 2)
        for h in range(2):
            for side in range(2):
                far_copy(h, side, j, o if side == 0 else -o, even if side == 0 else 1 - even)[
                    1
                ].wait_send()
        return carry

    lax.fori_loop(0, 3, far_done, 0)

    def members_done(r, carry):
        pred_copy(member(r))[1].wait_send()
        for v in range(2):
            gs_copy(v, r, my_share, member(-r)).wait_send()
        hr_copy(r).wait_send()
        return carry

    lax.fori_loop(1, 16, members_done, 0)

    def grad_done(j, carry):
        grad_copy(j).wait()
        return carry

    lax.fori_loop(0, 4, grad_done, 0)

    def ha_wait(r, carry):
        ha_copy(r, member(-r)).wait_recv()
        return carry

    lax.fori_loop(1, 16, ha_wait, 0)
    for j in range(16):
        lo = 24 * (j // 4)
        n = min(24, VARS - lo)
        head_out[lo : lo + n, 0, 128 * (j % 4) : 128 * (j % 4) + 128] = hall[j].astype(F32)[:n]


    def told(r, carry):
        ha_copy(r, me_m).wait_send()
        return carry

    lax.fori_loop(1, 16, told, 0)


def shards(
    coarse_latents,
    send_rows,
    up_index,
    up_weight,
    neighbors,
    live_counts,
    area,
    fine_skip,
    targets,
    kernel_width,
    w_in,
    w_out,
    ln_gain,
    w_head,
):
    hbm = pl.BlockSpec(memory_space=pl.ANY)
    vmem = pl.BlockSpec(memory_space=pltpu.VMEM)
    smem = pl.BlockSpec(memory_space=pltpu.SMEM)
    dma = pltpu.SemaphoreType.DMA
    grad_latent, head = pl.pallas_call(
        kernel,
        name="decoder_tail",
        out_shape=(
            jax.ShapeDtypeStruct((2048, 512), BF16),
            jax.ShapeDtypeStruct((VARS, 1, 512), F32),
        ),
        in_specs=[hbm] * 5 + [smem] + [hbm] * 8,
        out_specs=(hbm, vmem),
        scratch_shapes=[
            pltpu.VMEM((16, 128), jnp.int32),
            pltpu.VMEM((3, 2048), jnp.int32),
            pltpu.VMEM((3, 2048), F32),
            pltpu.VMEM((6, 2048), jnp.int32),
            pltpu.VMEM((1, 128), F32),
            pltpu.VMEM((VARS, 128), BF16),
            pltpu.VMEM((1, VARS), F32),
            pltpu.VMEM((1, 512), F32),
            pltpu.VMEM((VARS, 512), BF16),
            pltpu.VMEM((2, 5, 512, 256), BF16),
            pltpu.VMEM((4, 16, 128), jnp.int32),
            pltpu.VMEM((8, 2048, 512), BF16),
            pltpu.VMEM((2048, 512), BF16),
            pltpu.VMEM((6, 128, 128), F32),
            pltpu.VMEM((8, 256, 512), BF16),
            pltpu.VMEM((2, 2, 3, 128, 256), BF16),
            pltpu.VMEM((2, 5, 128, 256), BF16),
            pltpu.VMEM((2048, 512), F32),
            pltpu.VMEM((2048, 512), BF16),
            pltpu.VMEM((2304, 512), BF16),
            pltpu.VMEM((2048, 512), BF16),
            pltpu.VMEM((1024, 512), BF16),
            pltpu.VMEM((512, 512), BF16),
            pltpu.VMEM((VP, 512), BF16),
            pltpu.VMEM((8, 128), F32),
            pltpu.VMEM((VP, 128), F32),
            pltpu.VMEM((VP, 128), F32),
            pltpu.VMEM((16, VP, 128), BF16),
            pltpu.VMEM((16, VP, 128), BF16),
            pltpu.VMEM((16, VP, 128), F32),
            pltpu.VMEM((16, VP, 128), BF16),
            pltpu.VMEM((VP, 2048), BF16),
            pltpu.VMEM((16, 24, 128), BF16),
            pltpu.VMEM((16, 24, 128), BF16),
            pltpu.VMEM((24, 128), BF16),
            pltpu.VMEM((16, 24, 128), BF16),
            pltpu.SemaphoreType.REGULAR((7,)),
            dma((14,)),
            dma((4,)),
            dma((2, 4)),
            dma((2, 4)),
            dma((4,)),
            dma((4,)),
            dma((2, 2, 3)),
            dma((2, 5)),
            dma((2, 8, 2)),
            dma((2,)),
            dma((2,)),
            dma((16,)),
            dma((16,)),
            dma((2, 16)),
            dma((2, 16)),
            dma((16,)),
            dma((16,)),
            dma((16,)),
            dma((16,)),
        ],
        compiler_params=pltpu.CompilerParams(
            collective_id=0, has_side_effects=True, vmem_limit_bytes=60 * 1024 * 1024
        ),
    )(
        coarse_latents[0],
        send_rows[0],
        up_index,
        up_weight,
        neighbors,
        live_counts,
        area[None],
        fine_skip,
        targets,
        kernel_width[None],
        w_in,
        w_out,
        ln_gain[None],
        w_head.T,
    )
    return grad_latent[None], head.transpose(1, 2, 0)


def solution(mesh):
    in_specs = (
        P("mem", "dom", None),
        P("dom", None, None),
        P(None, "dom"),
        P(None, "dom"),
        P(None, "dom"),
        P("dom"),
        P("dom"),
        P("dom", None),
        P(None, "dom"),
        P(),
        P(),
        P(),
        P(),
        P(),
    )
    out_specs = (P("mem", "dom", None), P("dom", None, None))
    return jax.shard_map(
        shards, mesh=mesh, in_specs=in_specs, out_specs=out_specs, check_vma=False
    )
```

```python
import functools
import math

import jax
import jax.numpy as jnp
from jax import lax
from jax.experimental import pallas as pl
from jax.experimental.pallas import tpu as pltpu
from jax.sharding import PartitionSpec as P

F32 = jnp.float32
BF16 = jnp.bfloat16
VARS = 83
VP = 96
NT = (((1,), (1,)), ((), ()))


def lanes_of(row):
    return jnp.broadcast_to(row, (128, 128)).T


def kernel(
    coarse,
    send_rows,
    up_index_h,
    up_weight_h,
    neighbors_h,
    live,
    area_h,
    skip,
    targets_h,
    kwidth_h,
    w_in,
    w_out,
    gain_h,
    w_head_h,
    grad_out,
    head_out,
    own_rows,
    up_index,
    up_weight,
    neighbors,
    area,
    targets,
    kwidth,
    gain,
    w_head,
    tiles,
    rows,
    wbuf,
    nbuf,
    cols,
    recv,
    sbuf,
    sibbuf,
    acc,
    skipv,
    ext,
    hidden,
    win,
    wout,
    wht,
    kwp,
    inv_b,
    tgt,
    psend,
    pall,
    pf,
    ssend,
    gs,
    hp,
    hr,
    hs,
    hall,
    loc_sem,
    grad_sem,
    tile_s,
    tile_r,
    rows_s,
    rows_r,
    g_s,
    sib_s,
    recv_sem,
    rim_s,
    rim_r,
    pred_s,
    pred_r,
    gs_s,
    gs_r,
    hr_s,
    hr_r,
    ha_s,
    ha_r,
):
    me_d = lax.axis_index("dom")
    me_m = lax.axis_index("mem")
    c = me_d // 2
    k = me_d - 2 * c
    other = 1 - k

    def chip(offset):
        return lax.rem(c + offset + 8, 8)

    def member(offset):
        return lax.rem(me_m + offset + 16, 16)

    def remote(src, dst, ssem, rsem, **device):
        return pltpu.make_async_remote_copy(
            src_ref=src,
            dst_ref=dst,
            send_sem=ssem,
            recv_sem=rsem,
            device_id=device,
            device_id_type=pl.DeviceIdType.MESH,
        )

    barrier = pltpu.get_barrier_semaphore()

    def greet(r, carry):
        pl.semaphore_signal(
            barrier,
            inc=1,
            device_id={"dom": lax.rem(me_d + r, 16)},
            device_id_type=pl.DeviceIdType.MESH,
        )
        pl.semaphore_signal(
            barrier, inc=1, device_id={"mem": member(r)}, device_id_type=pl.DeviceIdType.MESH
        )
        return carry

    lax.fori_loop(1, 16, greet, 0)
    my_share = pl.ds(pl.multiple_of(me_m * 128, 128), 128)
    loads = [
        pltpu.make_async_copy(src, dst, loc_sem.at[i])
        for i, (src, dst) in enumerate(
            (
                (send_rows, own_rows),
                (coarse.at[:, :256], tiles.at[0, 0]),
                (coarse.at[:, 256:], tiles.at[1, 0]),
                (neighbors_h, neighbors),
                (w_head_h, w_head),
                (kwidth_h, kwidth),
                (targets_h.at[:, my_share], targets),
                (area_h.at[:, my_share], area),
                (up_index_h, up_index),
                (up_weight_h, up_weight),
                (gain_h, gain),
                (skip, skipv),
                (w_in, win),
                (w_out, wout),
            )
        )
    ]
    pl.semaphore_wait(barrier, 30)

    next_to = (chip(1) * 2 + k, chip(-1) * 2 + k)

    def pass_on(h, src, slot, side):
        return remote(
            src,
            tiles.at[h, slot],
            tile_s.at[h, slot - 1],
            tile_r.at[h, slot - 1],
            dom=next_to[side],
        )

    def pass_rows(src, slot, side):
        return remote(
            src,
            rows.at[slot - 1],
            rows_s.at[slot - 1],
            rows_r.at[slot - 1],
            dom=next_to[side],
        )

    row_copies = [pass_rows(send_rows, 1 + side, side) for side in range(2)]
    near = [
        [
            pass_on(h, coarse.at[:, 256 * h : 256 * h + 256], 1 + side, side)
            for side in range(2)
        ]
        for h in range(2)
    ]
    for copy in row_copies + near[0] + near[1]:
        copy.start()
    for load in loads:
        load.start()

    lane = lax.broadcasted_iota(jnp.int32, (128, 128), 1).astype(F32)

    def picked(table, tile, dest):
        row = table[pl.ds(dest, 1), :].astype(F32)
        col = lanes_of(row)
        hot = jnp.concatenate(
            [jnp.where(col == lane + 128.0 * q, 1.0, 0.0).astype(BF16) for q in range(4)], axis=1
        )
        return jnp.dot(hot, tile[...], preferred_element_type=F32).astype(BF16)

    my_rows = pl.ds(pl.multiple_of(k * 128, 128), 128)

    def at_home(table, slot, rel):
        for h in range(2):
            tile = tiles.at[h, slot]
            lanes = slice(256 * h, 256 * h + 256)
            sibbuf[h, slot] = picked(table, tile, me_d + other - k)
            copy = remote(
                sibbuf.at[h, slot],
                recv.at[rel, my_rows, lanes],
                sib_s.at[h, slot],
                recv_sem.at[h, rel, k],
                dom=c * 2 + other,
            )
            copy.start()
            recv[rel, my_rows, lanes] = picked(table, tile, me_d)
            sib_copies.append(copy)

    sib_copies = []
    for load in loads[:3]:
        load.wait()
    at_home(own_rows, 0, 0)

    def weights_of(t, carry):
        at = pl.ds(pl.multiple_of(t * 128, 128), 128)
        for j in range(3):
            cols[j] = lanes_of(up_index[j : j + 1, at].astype(F32))
            cols[3 + j] = lanes_of(up_weight[j : j + 1, at])

        def part(s, carry):
            sub = pl.ds(pl.multiple_of(s * 32, 32), 32)
            out = pl.ds(pl.multiple_of(t * 128 + s * 32, 32), 32)
            idx = [cols[j, sub, :] for j in range(3)]
            wgt = [cols[3 + j, sub, :] for j in range(3)]
            base = lax.broadcasted_iota(jnp.int32, (32, 128), 1).astype(F32)
            for q in range(16):
                slot = base + 128.0 * q
                w = (
                    jnp.where(idx[0] == slot, wgt[0], 0.0)
                    + jnp.where(idx[1] == slot, wgt[1], 0.0)
                    + jnp.where(idx[2] == slot, wgt[2], 0.0)
                )
                hi = w.astype(BF16)
                lo = (w - hi.astype(F32)).astype(BF16)
                wbuf[q // 2, out, (q % 2) * 128 : (q % 2) * 128 + 128] = hi
                wbuf[q // 2, out, 256 + (q % 2) * 128 : 384 + (q % 2) * 128] = lo
            return carry

        lax.fori_loop(0, 4, part, 0)
        return carry

    def counts_of(t, carry):
        at = pl.ds(pl.multiple_of(t * 128, 128), 128)
        shift = ((t // 2) * 256).astype(F32)
        for j in range(6):
            cols[j] = lanes_of(neighbors[j : j + 1, at].astype(F32) - shift)

        def part(s, carry):
            sub = pl.ds(pl.multiple_of(s * 32, 32), 32)
            out = pl.ds(pl.multiple_of(t * 128 + s * 32, 32), 32)
            idx = [cols[j, sub, :] for j in range(6)]
            base = lax.broadcasted_iota(jnp.int32, (32, 128), 1).astype(F32)
            for q in range(4):
                spot = base + 128.0 * q
                total = jnp.where(idx[0] == spot, 1.0, 0.0)
                for j in range(1, 6):
                    total = total + jnp.where(idx[j] == spot, 1.0, 0.0)
                nbuf[out, q * 128 : q * 128 + 128] = total.astype(BF16)
            return carry

        lax.fori_loop(0, 4, part, 0)
        return carry

    for load in loads[3:8]:
        load.wait()
    wht[...] = jnp.zeros((VP, 512), BF16)
    wht[:VARS, :] = w_head[...]
    kwp[...] = jnp.ones((8, 128), F32)
    kwp[0:1, :VARS] = kwidth[...]
    width = kwp[0:1, :]
    inv_b[...] = lanes_of(1.0 / (width * width))[:VP]
    tgt[...] = jnp.zeros((VP, 128), F32)
    tgt[:VARS, :] = targets[...].astype(F32)

    lax.fori_loop(0, 16, counts_of, 0)

    for copy in row_copies:
        copy.wait_recv()
    row_copies += [pass_rows(rows.at[side], 3 + side, side) for side in range(2)]
    for copy in row_copies[2:]:
        copy.start()
    next_one = []

    def forward(h):
        for side in range(2):
            near[h][side].wait_recv()
            copy = pass_on(h, tiles.at[h, 1 + side], 3 + side, side)
            copy.start()
            next_one.append(copy)

    forward(0)
    for load in loads[8:10]:
        load.wait()
    lax.fori_loop(0, 8, weights_of, 0)
    forward(1)
    at_home(rows.at[0], 1, 7)
    at_home(rows.at[1], 2, 1)
    lax.fori_loop(8, 16, weights_of, 0)
    for load in loads[10:]:
        load.wait()

    def far_copy(h, side, j, o, kd):
        dest = chip(o) * 2 + kd
        rel = 5 - j // 2 if side == 0 else 3 + j // 2
        return dest, remote(
            sbuf.at[h, side, j],
            recv.at[rel, my_rows, 256 * h : 256 * h + 256],
            g_s.at[h, side, j],
            recv_sem.at[h, rel, k],
            dom=dest,
        )

    def send_far(h):
        for copy in next_one[2 * h : 2 * h + 2]:
            copy.wait_recv()

        def both_ways(j, carry):
            o = 1 + j // 2
            even = lax.rem(j, 2)
            for side in range(2):
                dest, copy = far_copy(
                    h, side, j, o if side == 0 else -o, even if side == 0 else 1 - even
                )
                sbuf[h, side, j] = picked(rows.at[2 + side], tiles.at[h, 3 + side], dest)
                copy.start()
            return carry

        lax.fori_loop(0, 3, both_ways, 0)

    def arrived(rel, kb):
        half = pl.ds(pl.multiple_of(kb * 128, 128), 128)
        for h in range(2):
            remote(
                sibbuf.at[h, 0],
                recv.at[rel, half, 256 * h : 256 * h + 256],
                sib_s.at[h, 0],
                recv_sem.at[h, rel, kb],
                dom=c * 2 + other,
            ).wait_recv()

    def added(rels, t):
        at = pl.ds(pl.multiple_of(t * 512, 512), 512)
        total = skipv[at, :].astype(F32) if rels[0] == 0 else acc[at, :]
        for rel in rels:
            here = chip(rel)
            table = recv[rel]
            total = total + jnp.dot(wbuf[here, at, :256], table, preferred_element_type=F32)
            total = total + jnp.dot(wbuf[here, at, 256:], table, preferred_element_type=F32)
        return at, total

    def unpool(rels):
        for rel in rels:
            arrived(rel, other)
            if rel in (3, 4, 5):
                arrived(rel, k)

        def accumulate(t, carry, rels=rels):
            at, total = added(rels, t)
            acc[at, :] = total
            return carry

        lax.fori_loop(0, 4, accumulate, 0)

    for copy in row_copies[2:]:
        copy.wait_recv()
    send_far(0)
    unpool((0,))
    unpool((7, 1))
    send_far(1)
    at_home(rows.at[2], 3, 6)
    at_home(rows.at[3], 4, 2)
    unpool((6, 2))
    unpool((5, 3))
    arrived(4, 0)
    arrived(4, 1)

    def finish(t, carry):
        total = added((4,), t)[1]
        ext[pl.ds(pl.multiple_of(t * 512 + 128, 128), 512), :] = total.astype(BF16)
        return carry

    lax.fori_loop(0, 2, lambda t, carry: finish(t * 3, carry), 0)
    rims = [
        remote(
            ext.at[pl.ds(2048, 128)],
            ext.at[pl.ds(0, 128)],
            rim_s.at[0],
            rim_r.at[0],
            dom=lax.rem(me_d + 1, 16),
        ),
        remote(
            ext.at[pl.ds(128, 128)],
            ext.at[pl.ds(2176, 128)],
            rim_s.at[1],
            rim_r.at[1],
            dom=lax.rem(me_d + 15, 16),
        ),
    ]
    for rim in rims:
        rim.start()
    lax.fori_loop(1, 3, finish, 0)

    gain_row = gain[...]

    def pred_copy(j):
        r = lax.rem(j - me_m + 16, 16)
        return r, remote(psend.at[j], pall.at[r], pred_s.at[r], pred_r.at[r], mem=j)

    def dense(i, carry):
        x = ext[pl.ds(pl.multiple_of(i * 512 + 128, 128), 512), :]
        parts = []
        for s in range(2):
            start = pl.multiple_of(i * 512 + s * 256, 256)
            total = jnp.dot(
                nbuf[pl.ds(start, 256), :], ext[pl.ds(start, 512), :], preferred_element_type=F32
            )
            parts.append((total * (1.0 / 6)).astype(BF16))
        agg = jnp.concatenate(parts, axis=0)
        pre = jnp.dot(x, win[:512], preferred_element_type=F32) + jnp.dot(
            agg, win[512:], preferred_element_type=F32
        )
        half = 0.5 * pre
        act = (half + half * jnp.tanh(half)).astype(BF16)
        upd = jnp.dot(act, wout[...], preferred_element_type=F32)
        for g in range(2):
            u = upd[256 * g : 256 * g + 256]
            mean = jnp.sum(u, axis=1, keepdims=True) * (1.0 / 512)
            centred = u - mean
            var = jnp.sum(centred * centred, axis=1, keepdims=True) * (1.0 / 512)
            h = (
                x[256 * g : 256 * g + 256].astype(F32)
                + centred * lax.rsqrt(var + 1e-05) * gain_row
            ).astype(BF16)
            hidden[pl.ds(pl.multiple_of(i * 512 + 256 * g, 256), 256), :] = h
            pred = lax.dot_general(wht[...], h, NT, preferred_element_type=F32).astype(BF16)
            for s in range(2):
                j = 4 * i + 2 * g + s
                r, copy = pred_copy(j)
                psend[j] = pred[:, s * 128 : s * 128 + 128]

                @pl.when(r != 0)
                def _():
                    copy.start()

                @pl.when(r == 0)
                def _():
                    pall[0] = psend[j]

        return carry

    lax.fori_loop(1, 3, dense, 0)
    for rim in rims:
        rim.wait()

    @pl.when(me_d == 0)
    def _():
        ext[pl.ds(0, 128), :] = jnp.zeros((128, 512), BF16)

    @pl.when(me_d == 15)
    def _():
        ext[pl.ds(2176, 128), :] = jnp.zeros((128, 512), BF16)

    lax.fori_loop(0, 2, lambda t, carry: dense(t * 3, carry), 0)

    def pred_wait(r, carry):
        remote(psend.at[0], pall.at[r], pred_s.at[r], pred_r.at[r], mem=member(r)).wait_recv()
        return carry

    lax.fori_loop(1, 16, pred_wait, 0)

    def widen(r, carry):
        pf[r] = pall[r].astype(F32)
        return carry

    lax.fori_loop(0, 16, widen, 0)
    place = lax.broadcasted_iota(jnp.int32, (1, 128), 1) + me_m * 128
    weight = jnp.broadcast_to(jnp.where(place < live[0], area[...], 0.0), (8, 128))

    def scores(q, carry):
        at = pl.ds(pl.multiple_of(q * 8, 8), 8)
        inv = inv_b[at, :]
        halved = -0.5 * inv
        p = [pf[i, at, :] for i in range(16)]
        t = tgt[at, :]
        total = [None] * 16
        for i in range(16):
            for j in range(i):
                e = p[i] - p[j]
                s = e * jnp.exp(e * e * halved)
                total[i] = s if total[i] is None else total[i] + s
                total[j] = -s if total[j] is None else total[j] - s
        scale = weight * inv
        for i in range(16):
            e = p[i] - t
            pf[i, at, :] = scale * (e * jnp.exp(e * e * halved) - total[i] * (1.0 / 16))
        return carry


    def gs_copy(v, r, share, back):
        return remote(
            ssend.at[r, pl.ds(32 * v, 32)],
            gs.at[pl.ds(32 * v, 32), share],
            gs_s.at[v, r],
            gs_r.at[v, r],
            mem=back,
        )

    for v in range(3):
        lax.fori_loop(4 * v, min(4 * v + 4, -(-VARS // 8)), scores, 0)

        def give_back(r, carry, v=v):
            ssend[r, 32 * v : 32 * v + 32, :] = pf[r, 32 * v : 32 * v + 32, :].astype(BF16)
            gs_copy(v, r, my_share, member(-r)).start()
            return carry

        lax.fori_loop(1, 16, give_back, 0)
        gs[32 * v : 32 * v + 32, my_share] = pf[0, 32 * v : 32 * v + 32, :].astype(BF16)

    def gs_wait(r, carry):
        share = pl.ds(pl.multiple_of(member(r) * 128, 128), 128)
        for v in range(3):
            gs_copy(v, r, share, member(r)).wait_recv()
        return carry

    lax.fori_loop(1, 16, gs_wait, 0)

    head = jnp.dot(gs[...], hidden[...], preferred_element_type=F32)
    for j in range(16):
        lo, left = 24 * (j // 4), 128 * (j % 4)
        hp[j] = head[lo : lo + 24, left : left + 128].astype(BF16)

    def hr_copy(r):
        return remote(hp.at[member(r)], hr.at[r], hr_s.at[r], hr_r.at[r], mem=member(r))

    def spread(r, carry):
        hr_copy(r).start()
        return carry

    lax.fori_loop(1, 16, spread, 0)
    hr[0] = hp[me_m]

    def grad_copy(j):
        at = pl.ds(pl.multiple_of(j * 512, 512), 512)
        return pltpu.make_async_copy(skipv.at[at], grad_out.at[at], grad_sem.at[j])

    def gradient(j, carry):
        at = pl.ds(pl.multiple_of(j * 512, 512), 512)
        skipv[at, :] = lax.dot_general(
            gs[:, at], wht[...], (((0,), (0,)), ((), ())), preferred_element_type=F32
        ).astype(BF16)
        grad_copy(j).start()
        return carry

    lax.fori_loop(0, 4, gradient, 0)

    def hr_wait(r, carry):
        hr_copy(r).wait_recv()
        return carry

    lax.fori_loop(1, 16, hr_wait, 0)
    summed = hr[0].astype(F32)
    for r in range(1, 16):
        summed = summed + hr[r].astype(F32)
    summed = (summed * (1.0 / math.sqrt(32768))).astype(BF16)
    hs[...] = summed
    hall[me_m] = summed

    def ha_copy(r, owner):
        return remote(hs, hall.at[owner], ha_s.at[r], ha_r.at[r], mem=member(r))

    def tell(r, carry):
        ha_copy(r, me_m).start()
        return carry

    lax.fori_loop(1, 16, tell, 0)

    for copy in row_copies + near[0] + near[1] + next_one + sib_copies:
        copy.wait_send()

    def far_done(j, carry):
        o = 1 + j // 2
        even = lax.rem(j, 2)
        for h in range(2):
            for side in range(2):
                far_copy(h, side, j, o if side == 0 else -o, even if side == 0 else 1 - even)[
                    1
                ].wait_send()
        return carry

    lax.fori_loop(0, 3, far_done, 0)

    def members_done(r, carry):
        pred_copy(member(r))[1].wait_send()
        for v in range(3):
            gs_copy(v, r, my_share, member(-r)).wait_send()
        hr_copy(r).wait_send()
        return carry

    lax.fori_loop(1, 16, members_done, 0)

    def grad_done(j, carry):
        grad_copy(j).wait()
        return carry

    lax.fori_loop(0, 4, grad_done, 0)

    def ha_wait(r, carry):
        ha_copy(r, member(-r)).wait_recv()
        return carry

    lax.fori_loop(1, 16, ha_wait, 0)
    for j in range(16):
        lo = 24 * (j // 4)
        n = min(24, VARS - lo)
        head_out[lo : lo + n, 0, 128 * (j % 4) : 128 * (j % 4) + 128] = hall[j].astype(F32)[:n]


    def told(r, carry):
        ha_copy(r, me_m).wait_send()
        return carry

    lax.fori_loop(1, 16, told, 0)


def shards(
    coarse_latents,
    send_rows,
    up_index,
    up_weight,
    neighbors,
    live_counts,
    area,
    fine_skip,
    targets,
    kernel_width,
    w_in,
    w_out,
    ln_gain,
    w_head,
):
    hbm = pl.BlockSpec(memory_space=pl.ANY)
    vmem = pl.BlockSpec(memory_space=pltpu.VMEM)
    smem = pl.BlockSpec(memory_space=pltpu.SMEM)
    dma = pltpu.SemaphoreType.DMA
    grad_latent, head = pl.pallas_call(
        kernel,
        name="decoder_tail",
        out_shape=(
            jax.ShapeDtypeStruct((2048, 512), BF16),
            jax.ShapeDtypeStruct((VARS, 1, 512), F32),
        ),
        in_specs=[hbm] * 5 + [smem] + [hbm] * 8,
        out_specs=(hbm, vmem),
        scratch_shapes=[
            pltpu.VMEM((16, 128), jnp.int32),
            pltpu.VMEM((3, 2048), jnp.int32),
            pltpu.VMEM((3, 2048), F32),
            pltpu.VMEM((6, 2048), jnp.int32),
            pltpu.VMEM((1, 128), F32),
            pltpu.VMEM((VARS, 128), BF16),
            pltpu.VMEM((1, VARS), F32),
            pltpu.VMEM((1, 512), F32),
            pltpu.VMEM((VARS, 512), BF16),
            pltpu.VMEM((2, 5, 512, 256), BF16),
            pltpu.VMEM((4, 16, 128), jnp.int32),
            pltpu.VMEM((8, 2048, 512), BF16),
            pltpu.VMEM((2048, 512), BF16),
            pltpu.VMEM((6, 128, 128), F32),
            pltpu.VMEM((8, 256, 512), BF16),
            pltpu.VMEM((2, 2, 3, 128, 256), BF16),
            pltpu.VMEM((2, 5, 128, 256), BF16),
            pltpu.VMEM((2048, 512), F32),
            pltpu.VMEM((2048, 512), BF16),
            pltpu.VMEM((2304, 512), BF16),
            pltpu.VMEM((2048, 512), BF16),
            pltpu.VMEM((1024, 512), BF16),
            pltpu.VMEM((512, 512), BF16),
            pltpu.VMEM((VP, 512), BF16),
            pltpu.VMEM((8, 128), F32),
            pltpu.VMEM((VP, 128), F32),
            pltpu.VMEM((VP, 128), F32),
            pltpu.VMEM((16, VP, 128), BF16),
            pltpu.VMEM((16, VP, 128), BF16),
            pltpu.VMEM((16, VP, 128), F32),
            pltpu.VMEM((16, VP, 128), BF16),
            pltpu.VMEM((VP, 2048), BF16),
            pltpu.VMEM((16, 24, 128), BF16),
            pltpu.VMEM((16, 24, 128), BF16),
            pltpu.VMEM((24, 128), BF16),
            pltpu.VMEM((16, 24, 128), BF16),
            dma((14,)),
            dma((4,)),
            dma((2, 4)),
            dma((2, 4)),
            dma((4,)),
            dma((4,)),
            dma((2, 2, 3)),
            dma((2, 5)),
            dma((2, 8, 2)),
            dma((2,)),
            dma((2,)),
            dma((16,)),
            dma((16,)),
            dma((3, 16)),
            dma((3, 16)),
            dma((16,)),
            dma((16,)),
            dma((16,)),
            dma((16,)),
        ],
        compiler_params=pltpu.CompilerParams(
            collective_id=0, has_side_effects=True, vmem_limit_bytes=60 * 1024 * 1024
        ),
    )(
        coarse_latents[0],
        send_rows[0],
        up_index,
        up_weight,
        neighbors,
        live_counts,
        area[None],
        fine_skip,
        targets,
        kernel_width[None],
        w_in,
        w_out,
        ln_gain[None],
        w_head.T,
    )
    return grad_latent[None], head.transpose(1, 2, 0)


def solution(mesh):
    in_specs = (
        P("mem", "dom", None),
        P("dom", None, None),
        P(None, "dom"),
        P(None, "dom"),
        P(None, "dom"),
        P("dom"),
        P("dom"),
        P("dom", None),
        P(None, "dom"),
        P(),
        P(),
        P(),
        P(),
        P(),
    )
    out_specs = (P("mem", "dom", None), P("dom", None, None))
    return jax.shard_map(
        shards, mesh=mesh, in_specs=in_specs, out_specs=out_specs, check_vma=False
    )
```
